128 devices in a mesh: grp: 4 (over z), sub: 4 (over y), dev: 8 (over x, core).
Axes of the slice: x: 4, y: 4, z: 4, core: 2. Of those that a mesh axis runs over, the one named last changes fastest.
Arguments:
- queries: bfloat16 [4, 32, 512, 1024], P('grp', ('sub', 'dev')), may hold values from -8 to 8
- cached: bfloat16 [4, 32, 4096, 256], P('grp', ('sub', 'dev')), may hold values from -4.5 to 4.5
- new_entries: bfloat16 [4, 32, 512, 256], P('grp', ('sub', 'dev')), may hold values from -4.5 to 4.5
- lengths: int32 [32], P(('sub', 'dev')), may hold values from 1024 to 4096
- residual: bfloat16 [32, 512, 2048], P(('sub', 'dev'), 'grp'), may hold values from -6 to 6
- w_out: bfloat16 [4096, 2048], P('grp'), may hold values from -0.1875 to 0.1875
- norm_gain: float32 [2048], replicated, may hold values from 0.5 to 1.5
- w_gate_up: bfloat16 [128, 2048, 1536], P(('grp', 'sub', 'dev')), may hold values from -0.125 to 0.125
- w_down: bfloat16 [128, 768, 2048], P(('grp', 'sub', 'dev')), may hold values from -0.21875 to 0.21875
- routes: int32 [32, 512, 8], P(('sub', 'dev'), 'grp'), may hold values from 0 to 127, all different within a row; in each aligned block of 128 rows (0 to 127, 128 to 255, ..., all dimensions but the last counted through in order) at most 12 rows name the same one
- gate_codes: int32 [32, 512, 8], P(('sub', 'dev'), 'grp'), may hold values from 1 to 16
Outputs:
- attn_out: bfloat16 [32, 512, 2048], P(('sub', 'dev'), 'grp')
- mixed: bfloat16 [32, 512, 2048], P(('sub', 'dev'), 'grp')
The draws below stay inside these ranges and needn't reach their ends.
Inputs may be any that keep to these rules, and one draw needn't show every extreme that they name: `routes`: each row names 8 different experts; within the rows of one device (aligned blocks of 128 rows in the order of requests, then rows) no expert is named by more than 12 rows.
All inputs are finite; a program needn't handle non-finite values.
Results may differ from the reference program's by a relative error of at most 0.0052.
Values may be sent and summed in bfloat16 or wider, within the bound.
A program may use at most 128 MiB of HBM per device.

```python
import math
import jax
import jax.numpy as jnp
import numpy as np
from jax import lax

D = 2048
FF = 768
KVH = 4
HD = 128
TOP = 8
CACHE = 4096
ROWS = 512
GQ = 8
FEAT = 4096
EXPERTS = 128
REQS = 32
MOST = 12
N_GRP = 4
DEVICES = 128


def draw_queries(key, part):
    inner = jax.random.fold_in(key, 11)
    shape = (KVH, REQS, ROWS, GQ * HD)
    values = jnp.clip(2.5 * jax.random.normal(inner, shape, jnp.float32), -8.0, 8.0)
    return values.astype(jnp.bfloat16)


def draw_cached(key, part):
    inner = jax.random.fold_in(key, 23)
    shape = (KVH, REQS, CACHE, 2 * HD)
    values = jnp.clip(jax.random.normal(inner, shape, jnp.float32), -4.5, 4.5)
    return values.astype(jnp.bfloat16)


def set_ends(values, own_key, smallest, top_value):
    longest = values.shape.index(max(values.shape))
    spots = []
    for shift in (0, 1):
        where = [jax.random.randint(jax.random.fold_in(own_key, axis), (), 0, length) for axis, length in enumerate(values.shape)]
        where[longest] = (where[longest] + shift) % values.shape[longest]
        spots.append(tuple(where))
    return values.at[spots[0]].set(smallest).at[spots[1]].set(top_value)


def steps_of(key, shape, shards, least, high):
    loudness = 1.0
    for dim, blocks in shards:
        draws = jax.random.uniform(jax.random.fold_in(jax.random.fold_in(key, 6), dim), (blocks,), jnp.float32, least / len(shards), high / len(shards))
        loudness = loudness * jnp.repeat(jnp.exp(draws), shape[dim] // blocks).reshape((-1,) + (1,) * (len(shape) - 1 - dim))
    return loudness


def assign_block(own_key, own, number, rows, count, top, most, slope):
    sequence = jax.random.permutation(own_key, count)
    heavy_load, common = load_shares(count, rows * top, most, slope, True), load_shares(count, rows * top, most, slope, False)
    places = jnp.arange(count)

    def named(sizes, offset_by):
        used = int((sizes > 0).sum())
        fixed = max(1, used // 4)
        passed = fixed + (places - fixed + offset_by * (used - fixed)) % max(1, count - fixed)
        return jnp.zeros((count,), jnp.int32).at[sequence[jnp.where(places < fixed, places, passed)]].set(jnp.asarray(sizes, jnp.int32))

    sizes = jnp.where(number % 4 == 0, named(heavy_load, number // 4), named(common, number - number // 4 - 1))
    mixed = jax.random.permutation(jax.random.fold_in(own, 3), count)
    source_of, receiver = mixed[0:count // 2 * 2:2], mixed[1:count // 2 * 2:2]
    room = jnp.minimum(sizes[source_of] - 1, most - sizes[receiver]) // 2
    room = jnp.where((source_of == sequence[0]) | (receiver == sequence[0]) | (sizes[receiver] == 0), 0, jnp.maximum(room, 0))
    passed = jax.random.randint(jax.random.fold_in(own, 4), (count // 2,), 0, 1 << 20) % (room + 1)
    sizes = sizes.at[source_of].add(-passed).at[receiver].add(passed)
    items = jnp.searchsorted(jnp.cumsum(sizes), jnp.arange(rows * top), side="right").astype(jnp.int32)
    grid = items.reshape(top, rows).T
    grid = grid[jax.random.permutation(jax.random.fold_in(own, 1), rows)]
    offset_by = jax.random.randint(jax.random.fold_in(own, 2), (rows, 1), 0, top)
    return jnp.take_along_axis(grid, (jnp.arange(top)[None, :] + offset_by) % top, axis=1)


def load_shares(number_of, total, most, lean, full):
    portions = [(1 << 20) // math.isqrt(grade ** lean) + 1 for grade in range(1, number_of + 1)]
    largest = most if full else min(most, max(-(-total // number_of), total * portions[0] // sum(portions)))
    least = 1 if total - largest >= number_of - 1 else 0
    counts, rest = [largest] + [least] * (number_of - 1), total - largest - least * (number_of - 1)
    while rest > 0:
        candidates = [i for i in range(1, number_of) if counts[i] < largest] or [i for i in range(1, number_of) if counts[i] < most]
        pool, budget = sum([portions[i] for i in candidates]), rest
        for i in candidates:
            more = min(most - counts[i], max(1, budget * portions[i] // pool), rest)
            counts[i] = counts[i] + more
            rest = rest - more
    return np.array(counts)


def normal_values(key, dims, deviation, reach, pieces=(), kind=jnp.bfloat16):
    result = deviation * jax.random.normal(key, dims, jnp.float32)
    if pieces:
        result = result * steps_of(key, dims, pieces, -0.22, 0.18)
    return jnp.clip(result, -reach, reach).astype(kind)


def setup_inputs(seed: int = 0) -> dict:
    splits = jax.random.split(jax.random.key(seed), 12)
    queries = draw_queries(jax.random.fold_in(splits[11], 71), 0)
    cached = draw_cached(jax.random.fold_in(splits[11], 71), 0)
    new_entries = normal_values(splits[2], (KVH, REQS, ROWS, 2 * HD), 1.0, 4.5, ((0, 4), (1, 32)))
    lengths = set_ends(jax.random.randint(splits[3], (REQS,), CACHE // 4, CACHE + 1), jax.random.fold_in(splits[3], 1), CACHE // 4, CACHE).astype(jnp.int32)
    residual = normal_values(splits[4], (REQS, ROWS, D), 1.0, 6.0, ((0, 32), (1, 4)))
    w_out = normal_values(splits[5], (FEAT, D), (GQ * HD) ** -0.5, 0.1875, ((0, 4),))
    norm_gain = jnp.clip(1.0 + 0.1 * jax.random.normal(splits[6], (D,), jnp.float32), 0.5, 1.5)
    w_gate_up = normal_values(splits[7], (EXPERTS, D, 2 * FF), D ** -0.5, 0.125, ((0, 128),))
    w_down = normal_values(splits[8], (EXPERTS, FF, D), FF ** -0.5, 0.21875, ((0, 128),))
    routes_keys = jax.random.split(jax.random.fold_in(splits[9], 1), REQS * ROWS // (ROWS // N_GRP))
    routes_turns = jax.random.permutation(jax.random.fold_in(splits[9], 3), REQS * ROWS // (ROWS // N_GRP))
    routes = jax.vmap(lambda own, number: assign_block(jax.random.fold_in(splits[9], 2), own, number, ROWS // N_GRP, EXPERTS, TOP, MOST, 2))(routes_keys, routes_turns).reshape((REQS, ROWS, TOP))
    gate_codes = set_ends(jax.random.randint(splits[10], (REQS, ROWS, TOP), 1, 17), jax.random.fold_in(splits[10], 1), 1, 16).astype(jnp.int32)
    return {"queries": queries, "cached": cached, "new_entries": new_entries, "lengths": lengths, "residual": residual, "w_out": w_out, "norm_gain": norm_gain, "w_gate_up": w_gate_up, "w_down": w_down, "routes": routes, "gate_codes": gate_codes}


def attend(query_rows, cached_rows, entry_rows, length):
    head_width = cached_rows.shape[1] // 2
    stored = cached_rows.shape[0]
    span_len = entry_rows.shape[0]
    key_rows = jnp.concatenate([cached_rows[:, :head_width], entry_rows[:, :head_width]], axis=0)
    value_rows = jnp.concatenate([cached_rows[:, head_width:], entry_rows[:, head_width:]], axis=0)
    position = jnp.arange(stored + span_len, dtype=jnp.int32)[None, :]
    row_index = jnp.arange(span_len, dtype=jnp.int32)[:, None]
    visible = jnp.where(position < stored, position < length, position - stored <= row_index)
    head_queries = query_rows.reshape(span_len, -1, head_width).transpose(1, 0, 2)

    def one_head(head_rows):
        scores = jnp.dot(head_rows, key_rows.T, preferred_element_type=jnp.float32) * head_width ** (-0.5)
        scores = jnp.where(visible, scores, -1e+30)
        row_peak = lax.optimization_barrier(jnp.max(scores, axis=1, keepdims=True))
        exponent = jnp.exp(scores - row_peak)
        totals = lax.optimization_barrier(jnp.sum(exponent, axis=1, keepdims=True))
        weighted = jnp.dot(exponent.astype(jnp.bfloat16), value_rows, preferred_element_type=jnp.float32)
        return (weighted / totals).astype(jnp.bfloat16)
    outputs = lax.map(one_head, head_queries)
    return outputs.transpose(1, 0, 2).reshape(span_len, -1)

def reference(queries, cached, new_entries, lengths, residual, w_out, norm_gain, w_gate_up, w_down, routes, gate_codes):
    pair_count = KVH * REQS
    query_pairs = queries.reshape(pair_count, ROWS, -1)
    cache_pairs = cached.reshape(pair_count, CACHE, -1)
    entry_pairs = new_entries.reshape(pair_count, ROWS, -1)
    pair_lengths = jnp.tile(lengths, KVH).astype(jnp.int32)
    attended = lax.map(lambda packed: attend(packed[0], packed[1], packed[2], packed[3]), (query_pairs, cache_pairs, entry_pairs, pair_lengths))
    attended = attended.reshape(KVH, REQS * ROWS, -1)
    head_feat = attended.shape[2]
    attn_sum = jnp.zeros((REQS * ROWS, D), jnp.float32)
    for head_index in range(KVH):
        block = w_out[head_index * head_feat:(head_index + 1) * head_feat]
        attn_sum = attn_sum + jnp.dot(attended[head_index], block, preferred_element_type=jnp.float32)
    attn_out = attn_sum.astype(jnp.bfloat16).reshape(REQS, ROWS, D)
    state = residual.reshape(REQS * ROWS, D).astype(jnp.float32) + attn_sum
    scale_inv = lax.rsqrt(lax.optimization_barrier(jnp.mean(state * state, axis=1, keepdims=True)) + 1e-06)
    normed = (state * scale_inv * norm_gain.astype(jnp.float32)[None, :]).astype(jnp.bfloat16)
    codes_float = gate_codes.astype(jnp.float32)
    route_weight = codes_float / lax.optimization_barrier(jnp.sum(codes_float, axis=-1, keepdims=True))
    flat_routes = routes.reshape(-1).astype(jnp.int32)
    flat_weight = route_weight.reshape(-1)
    limit = DEVICES * MOST

    def per_expert(total, expert_id):
        chosen = flat_routes == expert_id
        hits = jnp.nonzero(chosen, size=limit, fill_value=0)[0].astype(jnp.int32)
        live = jnp.arange(limit, dtype=jnp.int32) < jnp.sum(chosen.astype(jnp.int32))
        token_ids = (hits // TOP).astype(jnp.int32)
        picked = normed[token_ids]
        projected = jnp.dot(picked, w_gate_up[expert_id], preferred_element_type=jnp.float32)
        expert_hidden = (jax.nn.silu(projected[:, :FF]) * projected[:, FF:]).astype(jnp.bfloat16)
        expert_out = lax.optimization_barrier(jnp.dot(expert_hidden, w_down[expert_id], preferred_element_type=jnp.float32).astype(jnp.bfloat16))
        weight = jnp.where(live, flat_weight[hits], 0.0)
        total = total.at[token_ids].add(expert_out.astype(jnp.float32) * weight[:, None])
        return (total, None)
    moe_total, _ = lax.scan(per_expert, jnp.zeros((REQS * ROWS, D), jnp.float32), jnp.arange(EXPERTS, dtype=jnp.int32))
    mixed = (state + moe_total).astype(jnp.bfloat16).reshape(REQS, ROWS, D)
    return (attn_out, mixed)
```

```python
import functools

import jax
import jax.numpy as jnp
from jax import lax
from jax.experimental import pallas as pl
from jax.experimental.pallas import tpu as pltpu
from jax.sharding import PartitionSpec as P

MESH = pl.DeviceIdType.MESH
TOP = 8
D = 2048
FF = 768
HD = 128
HEADS = 8
CACHE = 4096
SPAN = 512
KEYS = CACHE + SPAN
BLOCK = 128
UNIT = 512
TILE = 512
SCALE = HD**-0.5 * 1.4426950408889634
HIDDEN = -1e30
DEVICES = 128
STRIDE = 91
MSG = 8
MSG_COLS = D + D // 2
CHUNK = 32
CHUNKS = DEVICES // CHUNK
BF = jnp.bfloat16
F32 = jnp.float32


def iota(shape, dim):
    return lax.broadcasted_iota(jnp.int32, shape, dim)


def rem(a, b):
    return lax.rem(a, jnp.int32(b))


def div(a, b):
    return lax.div(a, jnp.int32(b))


def peer(slot, sign):
    g, s, d = lax.axis_index("grp"), lax.axis_index("sub"), lax.axis_index("dev")
    o = rem(slot * STRIDE, DEVICES)
    og, os, ox, oc = rem(o, 4), rem(div(o, 4), 4), rem(div(o, 16), 4), div(o, 64)
    x = rem(div(d, 2) + sign * ox + 4, 4)
    c = rem(rem(d, 2) + oc, 2)
    return rem(g + sign * og + 4, 4), rem(s + sign * os + 4, 4), x * 2 + c


def dot(a, b):
    return jnp.dot(a, b, preferred_element_type=F32)


def attend_kernel(
    length, q_ref, cached, new, residual, gain, w_hbm,
    out_ref, state_ref, normed_ref,
    keys, values, queries, scores, probs, peaks, attended, w_ref, sent, arrived, own,
    w_sem, send_sem, recv_sem,
):
    g, s, d = lax.axis_index("grp"), lax.axis_index("sub"), lax.axis_index("dev")
    w_copy = pltpu.make_async_copy(w_hbm, w_ref, w_sem)
    w_copy.start()
    barrier = pltpu.get_barrier_semaphore()
    for step in range(1, 4):
        pl.semaphore_signal(barrier, inc=1, device_id=(rem(g + step, 4), s, d), device_id_type=MESH)

    ones = jnp.where(iota((TILE, HD), 1) == 0, 1.0, 0.0).astype(BF)

    @pl.loop(0, CACHE // TILE)
    def _(i):
        rows = pl.ds(pl.multiple_of(i * TILE, TILE), TILE)
        keys[0:HD, rows] = cached[rows, 0:HD].T
        unseen = (iota((HD, TILE), 0) == 0) & (i * TILE + iota((HD, TILE), 1) >= length[0])
        keys[HD:, rows] = jnp.where(unseen, HIDDEN, 0.0).astype(BF)
        values[rows, 0:HD] = cached[rows, HD:]
        values[rows, HD:] = ones

    keys[0:HD, CACHE:] = new[:, 0:HD].T
    keys[HD:, CACHE:] = jnp.zeros((HD, SPAN), BF)
    values[CACHE:, 0:HD] = new[:, HD:]
    values[CACHE:, HD:] = ones
    for slot in range(2):
        queries[slot, :, HD:] = jnp.where(iota((UNIT, HD), 1) == 0, 1.0, 0.0).astype(BF)

    def score(step, slot):
        block = rem(g + 1 + step, 4)
        rows = pl.ds(pl.multiple_of(block * BLOCK, BLOCK), BLOCK)
        for k in range(4):
            head = slot * 4 + k
            queries[slot, k * BLOCK : (k + 1) * BLOCK, 0:HD] = q_ref[rows, head * HD : (head + 1) * HD]
        q = queries[slot]
        peak = None
        for j in range(KEYS // TILE):
            tile = dot(q, keys[:, j * TILE : (j + 1) * TILE])
            if j * TILE >= CACHE:
                row = block * BLOCK + rem(iota((UNIT, TILE), 0), BLOCK)
                tile = jnp.where(iota((UNIT, TILE), 1) + (j * TILE - CACHE) <= row, tile, HIDDEN)
            scores[slot, :, j * TILE : (j + 1) * TILE] = tile
            for k in range(TILE // HD):
                part = tile[:, k * HD : (k + 1) * HD]
                peak = part if peak is None else jnp.maximum(peak, part)
        peaks[slot] = jnp.broadcast_to(jnp.max(peak, axis=1, keepdims=True), (UNIT, HD))

    def finish(slot):
        peak = peaks[slot]
        for k in range(KEYS // HD):
            cols = slice(k * HD, (k + 1) * HD)
            probs[:, cols] = jnp.exp2((scores[slot, :, cols] - peak) * SCALE).astype(BF)
        total = dot(probs[...], values[...])
        result = (total[:, 0:HD] / total[:, HD : HD + 1]).astype(BF)
        for k in range(4):
            head = slot * 4 + k
            attended[:, head * HD : (head + 1) * HD] = result[k * BLOCK : (k + 1) * BLOCK]

    def hand_over(step):
        block = rem(g + 1 + step, 4)
        return pltpu.make_async_remote_copy(
            src_ref=sent.at[step], dst_ref=arrived.at[step],
            send_sem=send_sem.at[step], recv_sem=recv_sem.at[step],
            device_id=(block, s, d), device_id_type=MESH,
        )

    score(0, 0)
    w_copy.wait()
    pl.semaphore_wait(barrier, 3)

    @pl.loop(0, 4)
    def _(step):
        score(step, 1)
        finish(0)
        score(jnp.minimum(step + 1, 3), 0)
        finish(1)
        own[...] = dot(attended[...], w_ref[...])

        @pl.when(step < 3)
        def _():
            sent[step] = own[...].astype(BF)
            hand_over(step).start()

    for step in range(3):
        hand_over(step).wait()
    attn_sum = own[...] + (arrived[0].astype(F32) + (arrived[1].astype(F32) + arrived[2].astype(F32)))
    out_ref[...] = attn_sum.astype(BF)
    state = residual[...].astype(F32) + attn_sum
    state_ref[...] = state
    inverse = lax.rsqrt(jnp.mean(state * state, axis=1, keepdims=True) + 1e-6)
    normed_ref[...] = (state * inverse * gain[...]).astype(BF)


def attend_and_norm(length, queries, cached, new, residual, gain, w_out):
    vmem = pl.BlockSpec(memory_space=pltpu.VMEM)
    block = (BLOCK, D)
    return pl.pallas_call(
        attend_kernel,
        out_shape=(
            jax.ShapeDtypeStruct(block, BF),
            jax.ShapeDtypeStruct(block, F32),
            jax.ShapeDtypeStruct(block, BF),
        ),
        in_specs=[pl.BlockSpec(memory_space=pltpu.SMEM)] + [vmem] * 5 + [pl.BlockSpec(memory_space=pl.ANY)],
        out_specs=(vmem, vmem, vmem),
        scratch_shapes=[
            pltpu.VMEM((2 * HD, KEYS), BF),
            pltpu.VMEM((KEYS, 2 * HD), BF),
            pltpu.VMEM((2, UNIT, 2 * HD), BF),
            pltpu.VMEM((2, UNIT, KEYS), F32),
            pltpu.VMEM((UNIT, KEYS), BF),
            pltpu.VMEM((2, UNIT, HD), F32),
            pltpu.VMEM((BLOCK, HEADS * HD), BF),
            pltpu.VMEM((HEADS * HD, D), BF),
            pltpu.VMEM((3, *block), BF),
            pltpu.VMEM((3, *block), BF),
            pltpu.VMEM(block, F32),
            pltpu.SemaphoreType.DMA,
            pltpu.SemaphoreType.DMA((3,)),
            pltpu.SemaphoreType.DMA((3,)),
        ],
        compiler_params=pltpu.CompilerParams(
            collective_id=0, has_side_effects=True, vmem_limit_bytes=56 << 20
        ),
        name="attend_and_norm",
    )(length, queries, cached, new, residual, gain, w_out)


def expert_kernel(
    normed, state, slot_of, weight_of, up_hbm, down_hbm,
    mixed, recv, ret,
    send, back, w_up, w_down, x_ref, part, total,
    w_sem, send_sem, recv_sem, back_sem, ret_sem, part_sem,
):
    up_copy = pltpu.make_async_copy(up_hbm, w_up, w_sem.at[0])
    down_copy = pltpu.make_async_copy(down_hbm, w_down, w_sem.at[1])
    up_copy.start()
    down_copy.start()
    barrier = pltpu.get_barrier_semaphore()

    @pl.loop(1, DEVICES)
    def _(i):
        pl.semaphore_signal(barrier, inc=1, device_id=peer(i, 1), device_id_type=MESH)

    rows_of = CHUNK * MSG
    sub = rem(iota((rows_of, BLOCK), 0), MSG).astype(F32)
    first = sub < 4.0

    def peers_of(c):
        return pl.ds(c * CHUNK, CHUNK)

    def flat(ref, cols):
        part = ref[:, :, cols].astype(F32)
        return part.reshape(rows_of, part.shape[2]).astype(BF)

    def stacked(rows):
        return rows.reshape(CHUNK, MSG, rows.shape[1]).astype(BF)

    def spread(ref, c):
        rows = ref[pl.ds(pl.multiple_of(c * CHUNK, CHUNK), CHUNK), :]
        return jnp.broadcast_to(rows[:, None, :], (CHUNK, MSG, BLOCK)).reshape(rows_of, BLOCK)

    def hits(c):
        slot = spread(slot_of, c)
        return slot == sub, first & (slot == sub + 8.0), (~first) & (slot == sub + 4.0)

    def as_one(mask):
        return jnp.where(mask, 1.0, 0.0).astype(BF)

    def outbound(i, sign, source, target, s_sem, r_sem):
        c = div(i, CHUNK)
        return pltpu.make_async_remote_copy(
            src_ref=source.at[i], dst_ref=target.at[i],
            send_sem=s_sem.at[c], recv_sem=r_sem.at[c],
            device_id=peer(i, sign), device_id_type=MESH,
        )

    def to_self(source, target, sem):
        return pltpu.make_async_copy(source.at[0], target.at[0], sem.at[0])

    def start_all(c, sign, source, target, s_sem, r_sem):
        @pl.when(c == 0)
        def _():
            to_self(source, target, r_sem).start()

        @pl.loop(jnp.maximum(c * CHUNK, 1), (c + 1) * CHUNK)
        def _(i):
            outbound(i, sign, source, target, s_sem, r_sem).start()

    def take(c, source, sem):
        group = source.at[peers_of(c)]
        pltpu.make_async_copy(group, group, sem.at[c]).wait()
        copy = pltpu.make_async_copy(group, part, part_sem)
        copy.start()
        copy.wait()

    def fill(c):
        whole, low, high = hits(c)
        send[peers_of(c), :, 0:D] = stacked(dot(as_one(whole), normed[...]))
        halves = dot(as_one(low), normed[:, 0 : D // 2]) + dot(as_one(high), normed[:, D // 2 :])
        send[peers_of(c), :, D:] = stacked(halves)

    fill(0)
    pl.semaphore_wait(barrier, DEVICES - 1)
    start_all(0, 1, send, recv, send_sem, recv_sem)

    @pl.loop(1, CHUNKS)
    def _(c):
        fill(c)
        start_all(c, 1, send, recv, send_sem, recv_sem)

    up_copy.wait()
    down_copy.wait()
    quarter = CHUNK * 4
    r, k = iota((quarter, rows_of), 1), iota((quarter, rows_of), 0)
    where = div(k, 4) * MSG + rem(k, 4)
    pick_low, pick_high = as_one(r == where), as_one(r == where + 4)
    r, k = iota((rows_of, quarter), 0), iota((rows_of, quarter), 1)
    where = div(k, 4) * MSG + rem(k, 4)
    put_low, put_high = as_one(r == where), as_one(r == where + 4)

    @pl.loop(0, CHUNKS)
    def _(c):
        take(c, recv, recv_sem)
        x_ref[0:rows_of] = flat(part, slice(0, D))
        halves = flat(part, slice(D, MSG_COLS))
        x_ref[rows_of:, 0 : D // 2] = dot(pick_low, halves).astype(BF)
        x_ref[rows_of:, D // 2 :] = dot(pick_high, halves).astype(BF)
        projected = dot(x_ref[...], w_up[...])
        gate = projected[:, 0:FF]
        hidden = (gate / (1.0 + jnp.exp(-gate)) * projected[:, FF:]).astype(BF)
        result = dot(hidden, w_down[...])
        back[peers_of(c), :, 0:D] = stacked(result[0:rows_of])
        rest = result[rows_of:].astype(BF)
        back[peers_of(c), :, D:] = stacked(dot(put_low, rest[:, 0 : D // 2]) + dot(put_high, rest[:, D // 2 :]))
        start_all(c, -1, back, ret, back_sem, ret_sem)

    total[...] = state[...]

    def weighted(mask, weight):
        exact = jnp.where(mask, weight, 0.0)
        high = exact.astype(BF)
        return high, (exact - high.astype(F32)).astype(BF)

    def turned(a, b):
        return lax.dot_general(a, b, (((0,), (0,)), ((), ())), preferred_element_type=F32)

    @pl.loop(0, CHUNKS)
    def _(c):
        take(c, ret, ret_sem)
        weight = spread(weight_of, c)
        whole, low, high = hits(c)
        for mask, source, target in (
            (whole, slice(0, D), slice(0, D)),
            (low, slice(D, MSG_COLS), slice(0, D // 2)),
            (high, slice(D, MSG_COLS), slice(D // 2, D)),
        ):
            coarse, fine = weighted(mask, weight)
            rows = flat(part, source)
            total[:, target] += turned(coarse, rows) + turned(fine, rows)

    mixed[...] = total[...].astype(BF)
    for c in range(CHUNKS):
        rows = pl.ds(1 if c == 0 else c * CHUNK, CHUNK - (1 if c == 0 else 0))
        pltpu.make_async_copy(send.at[rows], send.at[rows], send_sem.at[c]).wait()
        pltpu.make_async_copy(back.at[rows], back.at[rows], back_sem.at[c]).wait()


def experts(normed, state, slot_of, weight_of, w_gate_up, w_down):
    vmem = pl.BlockSpec(memory_space=pltpu.VMEM)
    hbm = pl.BlockSpec(memory_space=pl.ANY)
    messages = (DEVICES, MSG, MSG_COLS)
    sems = pltpu.SemaphoreType.DMA((CHUNKS,))
    return pl.pallas_call(
        expert_kernel,
        out_shape=(
            jax.ShapeDtypeStruct((BLOCK, D), BF),
            jax.ShapeDtypeStruct(messages, BF),
            jax.ShapeDtypeStruct(messages, BF),
        ),
        in_specs=[vmem] * 4 + [hbm] * 2,
        out_specs=(vmem, hbm, hbm),
        scratch_shapes=[
            pltpu.VMEM(messages, BF),
            pltpu.VMEM(messages, BF),
            pltpu.VMEM((D, 2 * FF), BF),
            pltpu.VMEM((FF, D), BF),
            pltpu.VMEM((CHUNK * 12, D), BF),
            pltpu.VMEM((CHUNK, MSG, MSG_COLS), BF),
            pltpu.VMEM((BLOCK, D), F32),
            pltpu.SemaphoreType.DMA((2,)),
            sems, sems, sems, sems,
            pltpu.SemaphoreType.DMA,
        ],
        compiler_params=pltpu.CompilerParams(
            collective_id=1, has_side_effects=True, vmem_limit_bytes=56 << 20
        ),
        name="experts",
    )(normed, state, slot_of, weight_of, w_gate_up, w_down)[0]


def slots(routes, gate_codes):
    slot = jnp.arange(DEVICES, dtype=jnp.int32)
    g, s, d = peer(slot, 1)
    expert = (g * 32 + s * 8 + d)[:, None]
    codes = gate_codes.astype(F32)
    weight = (codes / jnp.sum(codes, axis=-1, keepdims=True)).T
    chosen = routes.T
    hit = jnp.zeros((DEVICES, BLOCK), jnp.bool_)
    weight_of = jnp.zeros((DEVICES, BLOCK), F32)
    for j in range(TOP):
        here = chosen[j][None, :] == expert
        hit = hit | here
        weight_of = weight_of + jnp.where(here, weight[j][None, :], 0.0)
    earlier = (iota((BLOCK, BLOCK), 0) < iota((BLOCK, BLOCK), 1)).astype(BF)
    rank = dot(hit.astype(BF), earlier)
    return jnp.where(hit, rank, -1.0), weight_of


def per_device(
    queries, cached, new_entries, lengths, residual, w_out, norm_gain, w_gate_up, w_down, routes, gate_codes
):
    slot_of, weight_of = slots(routes[0], gate_codes[0])
    attn_out, state, normed = attend_and_norm(
        lengths, queries[0, 0], cached[0, 0], new_entries[0, 0], residual[0], norm_gain[None, :], w_out
    )
    mixed = experts(normed, state, slot_of, weight_of, w_gate_up[0], w_down[0])
    return attn_out[None], mixed[None]


def solution(mesh):
    rows = P(("sub", "dev"), "grp", None)
    heads = P("grp", ("sub", "dev"), None, None)
    expert = P(("grp", "sub", "dev"), None, None)
    placed = (
        heads, heads, heads, P(("sub", "dev")), rows, P("grp", None), P(), expert, expert, rows, rows,
    )
    return jax.shard_map(per_device, mesh=mesh, in_specs=placed, out_specs=(rows, rows), check_vma=False)
```

```python
import functools

import jax
import jax.numpy as jnp
from jax import lax
from jax.experimental import pallas as pl
from jax.experimental.pallas import tpu as pltpu
from jax.sharding import PartitionSpec as P

MESH = pl.DeviceIdType.MESH
TOP = 8
D = 2048
FF = 768
HD = 128
HEADS = 8
CACHE = 4096
SPAN = 512
KEYS = CACHE + SPAN
BLOCK = 128
UNIT = 512
TILE = 512
SCALE = HD**-0.5 * 1.4426950408889634
HIDDEN = -1e30
DEVICES = 128
PLANE = 32
LINE = 4
AXES = 3
STRIDE = 11
MSG = 8
PARTS = ((0, 640), (640, 640), (1280, 768))
LOW = 384
CHUNK = 32
CHUNKS = DEVICES // CHUNK
BF = jnp.bfloat16
F32 = jnp.float32


def iota(shape, dim):
    return lax.broadcasted_iota(jnp.int32, shape, dim)


def rem(a, b):
    return lax.rem(a, jnp.int32(b))


def div(a, b):
    return lax.div(a, jnp.int32(b))


def place(offset, sign):
    g, s, d = lax.axis_index("grp"), lax.axis_index("sub"), lax.axis_index("dev")
    og, os, ox, oc = offset
    x = rem(div(d, 2) + sign * ox + 4, 4)
    return rem(g + sign * og + 4, 4), rem(s + sign * os + 4, 4), x * 2 + rem(rem(d, 2) + oc, 2)


def along(axis, step):
    return tuple(step if k == axis else 0 for k in range(AXES)) + (0,)


def across(axis, p):
    a, b, c = div(p, 8), rem(div(p, 2), 4), rem(p, 2)
    return ((0, a, b, c), (a, 0, b, c), (a, b, 0, c))[axis]


def source_at(axis, member, p):
    if axis == 0:
        return member * 32 + p
    if axis == 1:
        return div(p, 8) * 32 + member * 8 + rem(p, 8)
    return div(p, 2) * 8 + member * 2 + rem(p, 2)


def member_and_place(axis, source):
    if axis == 0:
        return div(source, 32), rem(source, 32)
    if axis == 1:
        return rem(div(source, 8), 4), div(source, 32) * 8 + rem(source, 8)
    return rem(div(source, 2), 4), div(source, 8) * 2 + rem(source, 2)


def mixed_place(step):
    o = rem(step * STRIDE, PLANE)
    return rem(o, 4) * 8 + rem(div(o, 4), 4) * 2 + div(o, 16)


def dot(a, b):
    return jnp.dot(a, b, preferred_element_type=F32)


def attend_kernel(
    length, q_ref, cached, new, residual, gain, choices, w_hbm,
    out_ref, state_ref, normed_ref, slot_of, weight_of,
    keys, values, queries, scores, probs, peaks, attended, w_ref, sent, arrived, own, lines,
    w_sem, send_sem, recv_sem, line_send, line_recv,
):
    g, s, d = lax.axis_index("grp"), lax.axis_index("sub"), lax.axis_index("dev")
    w_copy = pltpu.make_async_copy(w_hbm, w_ref, w_sem)
    w_copy.start()
    barrier = pltpu.get_barrier_semaphore()
    for axis in range(AXES):
        for step in range(1, LINE):
            pl.semaphore_signal(barrier, inc=1, device_id=place(along(axis, step), 1), device_id_type=MESH)

    ones = jnp.where(iota((TILE, HD), 1) == 0, 1.0, 0.0).astype(BF)

    @pl.loop(0, CACHE // TILE)
    def _(i):
        rows = pl.ds(pl.multiple_of(i * TILE, TILE), TILE)
        keys[0:HD, rows] = cached[rows, 0:HD].T
        unseen = (iota((HD, TILE), 0) == 0) & (i * TILE + iota((HD, TILE), 1) >= length[0])
        keys[HD:, rows] = jnp.where(unseen, HIDDEN, 0.0).astype(BF)
        values[rows, 0:HD] = cached[rows, HD:]
        values[rows, HD:] = ones

    keys[0:HD, CACHE:] = new[:, 0:HD].T
    keys[HD:, CACHE:] = jnp.zeros((HD, SPAN), BF)
    values[CACHE:, 0:HD] = new[:, HD:]
    values[CACHE:, HD:] = ones
    for slot in range(2):
        queries[slot, :, HD:] = jnp.where(iota((UNIT, HD), 1) == 0, 1.0, 0.0).astype(BF)

    def score(step, slot):
        block = rem(g + 1 + step, 4)
        rows = pl.ds(pl.multiple_of(block * BLOCK, BLOCK), BLOCK)
        for k in range(4):
            head = slot * 4 + k
            queries[slot, k * BLOCK : (k + 1) * BLOCK, 0:HD] = q_ref[rows, head * HD : (head + 1) * HD]
        q = queries[slot]
        peak = None
        for j in range(KEYS // TILE):
            tile = dot(q, keys[:, j * TILE : (j + 1) * TILE])
            if j * TILE >= CACHE:
                row = block * BLOCK + rem(iota((UNIT, TILE), 0), BLOCK)
                tile = jnp.where(iota((UNIT, TILE), 1) + (j * TILE - CACHE) <= row, tile, HIDDEN)
            scores[slot, :, j * TILE : (j + 1) * TILE] = tile
            for k in range(TILE // HD):
                part = tile[:, k * HD : (k + 1) * HD]
                peak = part if peak is None else jnp.maximum(peak, part)
        peaks[slot] = jnp.broadcast_to(jnp.max(peak, axis=1, keepdims=True), (UNIT, HD))

    def finish(slot):
        peak = peaks[slot]
        for k in range(KEYS // HD):
            cols = slice(k * HD, (k + 1) * HD)
            probs[:, cols] = jnp.exp2((scores[slot, :, cols] - peak) * SCALE).astype(BF)
        total = dot(probs[...], values[...])
        result = (total[:, 0:HD] / total[:, HD : HD + 1]).astype(BF)
        for k in range(4):
            head = slot * 4 + k
            attended[:, head * HD : (head + 1) * HD] = result[k * BLOCK : (k + 1) * BLOCK]

    def hand_over(step):
        block = rem(g + 1 + step, 4)
        return pltpu.make_async_remote_copy(
            src_ref=sent.at[step], dst_ref=arrived.at[step],
            send_sem=send_sem.at[step], recv_sem=recv_sem.at[step],
            device_id=(block, s, d), device_id_type=MESH,
        )

    def tell(axis, member):
        at = axis * (LINE - 1) + member - 1
        return pltpu.make_async_remote_copy(
            src_ref=choices, dst_ref=lines.at[at],
            send_sem=line_send.at[at], recv_sem=line_recv.at[at],
            device_id=place(along(axis, member), 1), device_id_type=MESH,
        )

    pairs = [(axis, member) for axis in range(AXES) for member in range(1, LINE)]
    score(0, 0)
    w_copy.wait()
    pl.semaphore_wait(barrier, len(pairs))
    for axis, member in pairs:
        tell(axis, member).start()

    @pl.loop(0, 4)
    def _(step):
        score(step, 1)
        finish(0)
        score(jnp.minimum(step + 1, 3), 0)
        finish(1)
        own[...] = dot(attended[...], w_ref[...])

        @pl.when(step < 3)
        def _():
            sent[step] = own[...].astype(BF)
            hand_over(step).start()

    for axis, member in pairs:
        tell(axis, member).wait()
    earlier = jnp.where(iota((BLOCK, BLOCK), 0) < iota((BLOCK, BLOCK), 1), 1.0, 0.0).astype(BF)
    p = iota((PLANE, BLOCK), 0)
    a, b, core = p >> 3, (p >> 1) & 3, (p + d) & 1
    x = div(d, 2)
    for axis in range(AXES):
        z, y, w = ((0, a, b), (a, 0, b), (a, b, 0))[axis]
        expert = (((g + z) & 3) * 32 + ((s + y) & 3) * 8 + ((x + w) & 3) * 2 + core).astype(F32)
        for member in range(LINE):
            chosen = choices[...] if member == 0 else lines[axis * (LINE - 1) + member - 1]
            hit = jnp.zeros((PLANE, BLOCK), F32)
            weight = jnp.zeros((PLANE, BLOCK), F32)
            for j in range(TOP):
                here = chosen[j : j + 1] == expert
                hit = jnp.where(here, 1.0, hit)
                weight = jnp.where(here, chosen[TOP + j : TOP + j + 1], weight)
            rows = slice((axis * LINE + member) * PLANE, (axis * LINE + member + 1) * PLANE)
            slot_of[rows] = jnp.where(hit > 0.0, dot(hit.astype(BF), earlier), -1.0)
            weight_of[rows] = weight
    for step in range(3):
        hand_over(step).wait()
    attn_sum = own[...] + (arrived[0].astype(F32) + (arrived[1].astype(F32) + arrived[2].astype(F32)))
    out_ref[...] = attn_sum.astype(BF)
    state = residual[...].astype(F32) + attn_sum
    state_ref[...] = state
    inverse = lax.rsqrt(jnp.mean(state * state, axis=1, keepdims=True) + 1e-6)
    normed_ref[...] = (state * inverse * gain[...]).astype(BF)


def attend_and_norm(length, queries, cached, new, residual, gain, choices, w_out):
    vmem = pl.BlockSpec(memory_space=pltpu.VMEM)
    block = (BLOCK, D)
    return pl.pallas_call(
        attend_kernel,
        out_shape=(
            jax.ShapeDtypeStruct(block, BF),
            jax.ShapeDtypeStruct(block, F32),
            jax.ShapeDtypeStruct(block, BF),
            jax.ShapeDtypeStruct((AXES * LINE * PLANE, BLOCK), F32),
            jax.ShapeDtypeStruct((AXES * LINE * PLANE, BLOCK), F32),
        ),
        in_specs=[pl.BlockSpec(memory_space=pltpu.SMEM)] + [vmem] * 6 + [pl.BlockSpec(memory_space=pl.ANY)],
        out_specs=(vmem,) * 5,
        scratch_shapes=[
            pltpu.VMEM((2 * HD, KEYS), BF),
            pltpu.VMEM((KEYS, 2 * HD), BF),
            pltpu.VMEM((2, UNIT, 2 * HD), BF),
            pltpu.VMEM((2, UNIT, KEYS), F32),
            pltpu.VMEM((UNIT, KEYS), BF),
            pltpu.VMEM((2, UNIT, HD), F32),
            pltpu.VMEM((BLOCK, HEADS * HD), BF),
            pltpu.VMEM((HEADS * HD, D), BF),
            pltpu.VMEM((3, *block), BF),
            pltpu.VMEM((3, *block), BF),
            pltpu.VMEM(block, F32),
            pltpu.VMEM((AXES * (LINE - 1), 2 * TOP, BLOCK), F32),
            pltpu.SemaphoreType.DMA,
            pltpu.SemaphoreType.DMA((3,)),
            pltpu.SemaphoreType.DMA((3,)),
            pltpu.SemaphoreType.DMA((AXES * (LINE - 1),)),
            pltpu.SemaphoreType.DMA((AXES * (LINE - 1),)),
        ],
        compiler_params=pltpu.CompilerParams(
            collective_id=0, has_side_effects=True, vmem_limit_bytes=56 << 20
        ),
        name="attend_and_norm",
    )(length, queries, cached, new, residual, gain, choices, w_out)


def expert_kernel(
    normed, state, slot_of, weight_of, up_hbm, down_hbm,
    mixed, recv0, recv1, recv2, ret0, ret1, ret2,
    send0, send1, send2, back0, back1, back2, line0, line1, line2, part0, part1, part2,
    out0, out1, out2, in0, in1, in2, w_up, w_down, x_ref, total,
    w_sem, line_send, line_recv, send_sem, recv_sem, back_sem, ret_sem, part_sem, out_sem, in_sem,
):
    recv, ret, send, back = (recv0, recv1, recv2), (ret0, ret1, ret2), (send0, send1, send2), (back0, back1, back2)
    line, part, leaving, coming = (line0, line1, line2), (part0, part1, part2), (out0, out1, out2), (in0, in1, in2)
    up_copy = pltpu.make_async_copy(up_hbm, w_up, w_sem.at[0])
    down_copy = pltpu.make_async_copy(down_hbm, w_down, w_sem.at[1])
    up_copy.start()
    down_copy.start()
    barrier = pltpu.get_barrier_semaphore()

    @pl.loop(1, DEVICES)
    def _(i):
        offset = (div(i, 32), rem(div(i, 8), 4), rem(div(i, 2), 4), rem(i, 2))
        pl.semaphore_signal(barrier, inc=1, device_id=place(offset, 1), device_id_type=MESH)

    rows_of = CHUNK * MSG
    sub = rem(iota((rows_of, BLOCK), 0), MSG).astype(F32)
    first = sub < 4.0
    for axis, (start, cols) in enumerate(PARTS):
        line[axis][0] = normed[:, start : start + cols]

    def flat(values):
        return values.astype(F32).reshape(rows_of, values.shape[2]).astype(BF)

    def stacked(rows):
        return rows.reshape(CHUNK, MSG, rows.shape[1]).astype(BF)

    def widened(rows):
        if rows.shape[1] == LOW:
            return rows
        return jnp.concatenate([rows, jnp.zeros((rows.shape[0], LOW - rows.shape[1]), F32)], axis=1)

    def spread(ref, axis, member):
        rows = ref[pl.ds(pl.multiple_of((axis * LINE + member) * PLANE, PLANE), PLANE), :]
        return jnp.broadcast_to(rows[:, None, :], (PLANE, MSG, BLOCK)).reshape(rows_of, BLOCK)

    def hits(axis, member):
        slot = spread(slot_of, axis, member)
        return slot == sub, first & (slot == sub + 8.0), (~first) & (slot == sub + 4.0)

    def as_one(mask):
        return jnp.where(mask, 1.0, 0.0).astype(BF)

    def share(axis, member):
        at = axis * (LINE - 1) + member - 1
        return pltpu.make_async_remote_copy(
            src_ref=line[axis].at[0], dst_ref=line[axis].at[member],
            send_sem=line_send.at[at], recv_sem=line_recv.at[at],
            device_id=place(along(axis, member), 1), device_id_type=MESH,
        )

    def outward(axis, member, p):
        return pltpu.make_async_remote_copy(
            src_ref=send[axis].at[member, p], dst_ref=recv[axis].at[source_at(axis, member, p)],
            send_sem=send_sem.at[axis], recv_sem=recv_sem.at[axis],
            device_id=place(across(axis, p), 1), device_id_type=MESH,
        )

    def homeward(axis, source):
        member, p = member_and_place(axis, source)
        return p, pltpu.make_async_remote_copy(
            src_ref=back[axis].at[source], dst_ref=ret[axis].at[member, p],
            send_sem=back_sem.at[axis], recv_sem=ret_sem.at[axis * LINE + member],
            device_id=place(across(axis, p), -1), device_id_type=MESH,
        ), pltpu.make_async_copy(
            back[axis].at[source], ret[axis].at[member, p], ret_sem.at[axis * LINE + member]
        )

    def go_home(axis, source):
        p, away, here = homeward(axis, source)

        @pl.when(p > 0)
        def _():
            away.start()

        @pl.when(p == 0)
        def _():
            here.start()

    def settle(axis, member):
        at = axis * (LINE - 1) + member - 1
        return pltpu.make_async_remote_copy(
            src_ref=leaving[axis].at[member - 1], dst_ref=coming[axis].at[member - 1],
            send_sem=out_sem.at[at], recv_sem=in_sem.at[at],
            device_id=place(along(axis, member), -1), device_id_type=MESH,
        )

    def take(sources):
        copies = [pltpu.make_async_copy(source, part[axis], part_sem.at[axis]) for axis, source in sources]
        for copy in copies:
            copy.start()
        for copy in copies:
            copy.wait()

    pl.semaphore_wait(barrier, DEVICES - 1)
    for member in range(1, LINE):
        for axis in range(AXES):
            share(axis, member).start()

    @pl.loop(0, LINE)
    def _(member):
        @pl.when(member > 0)
        def _():
            for axis in range(AXES):
                share(axis, member).wait_recv()

        for axis, (start, cols) in enumerate(PARTS):
            whole, low, high = hits(axis, member)
            rows = line[axis][member]
            send[axis][member, :, :, 0:cols] = stacked(dot(as_one(whole), rows))
            rest = dot(as_one(low), rows[:, 0:LOW]) + widened(dot(as_one(high), rows[:, LOW:]))
            send[axis][member, :, :, cols:] = stacked(rest)
            pltpu.make_async_copy(
                send[axis].at[member, 0], recv[axis].at[source_at(axis, member, 0)], recv_sem.at[axis]
            ).start()

        @pl.loop(1, PLANE)
        def _(step):
            p = mixed_place(step)
            for axis in range(AXES):
                outward(axis, member, p).start()

    up_copy.wait()
    down_copy.wait()
    total[...] = state[...]
    quarter = CHUNK * 4
    r, k = iota((quarter, rows_of), 1), iota((quarter, rows_of), 0)
    where = (k >> 2) * MSG + (k & 3)
    pick_low, pick_high = as_one(r == where), as_one(r == where + 4)
    r, k = iota((rows_of, quarter), 0), iota((rows_of, quarter), 1)
    where = (k >> 2) * MSG + (k & 3)
    put_low, put_high = as_one(r == where), as_one(r == where + 4)
    for axis in range(AXES):
        pltpu.make_async_copy(recv[axis], recv[axis], recv_sem.at[axis]).wait()

    @pl.loop(0, CHUNKS)
    def _(c):
        take([(axis, recv[axis].at[pl.ds(c * CHUNK, CHUNK)]) for axis in range(AXES)])
        for axis, (start, cols) in enumerate(PARTS):
            x_ref[0:rows_of, start : start + cols] = flat(part[axis][:, :, 0:cols])
            rest = flat(part[axis][:, :, cols:])
            x_ref[rows_of:, start : start + LOW] = dot(pick_low, rest).astype(BF)
            x_ref[rows_of:, start + LOW : start + cols] = dot(pick_high, rest[:, 0 : cols - LOW]).astype(BF)
        projected = dot(x_ref[...], w_up[...])
        gate = projected[:, 0:FF]
        hidden = (gate / (1.0 + jnp.exp(-gate)) * projected[:, FF:]).astype(BF)
        result = dot(hidden, w_down[...])
        cut = result[rows_of:].astype(BF)
        for axis, (start, cols) in enumerate(PARTS):
            back[axis][pl.ds(c * CHUNK, CHUNK), :, 0:cols] = stacked(result[0:rows_of, start : start + cols])
            rest = dot(put_low, cut[:, start : start + LOW])
            rest = rest + widened(dot(put_high, cut[:, start + LOW : start + cols]))
            back[axis][pl.ds(c * CHUNK, CHUNK), :, cols:] = stacked(rest)

        @pl.loop(0, PLANE)
        def _(step):
            source = c * CHUNK + mixed_place(step)
            for axis in range(AXES):
                member = member_and_place(axis, source)[0]

                @pl.when(member > 0)
                def _():
                    go_home(axis, source)

    @pl.loop(0, PLANE)
    def _(step):
        p = mixed_place(step)
        for axis in range(AXES):
            go_home(axis, source_at(axis, 0, p))

    def combine(axis, member):
        cols = PARTS[axis][1]
        group = ret[axis].at[member]
        pltpu.make_async_copy(group, group, ret_sem.at[axis * LINE + member]).wait()
        take([(axis, group)])
        weight = spread(weight_of, axis, member)

        def summed(mask, rows):
            exact = jnp.where(mask, weight, 0.0)
            coarse = exact.astype(BF)
            fine = (exact - coarse.astype(F32)).astype(BF)
            both = jnp.concatenate([coarse, fine], axis=1)
            out = lax.dot_general(both, rows, (((0,), (0,)), ((), ())), preferred_element_type=F32)
            return out[0:BLOCK] + out[BLOCK:]

        whole, low, high = hits(axis, member)
        rest = flat(part[axis][:, :, cols:])
        halves = jnp.concatenate([summed(low, rest), summed(high, rest[:, 0 : cols - LOW])], axis=1)
        return summed(whole, flat(part[axis][:, :, 0:cols])) + halves

    @pl.loop(1, LINE)
    def _(member):
        for axis in range(AXES):
            leaving[axis][member - 1] = combine(axis, member).astype(BF)
            settle(axis, member).start()

    for axis, (start, cols) in enumerate(PARTS):
        total[:, start : start + cols] += combine(axis, 0)

    for axis, (start, cols) in enumerate(PARTS):
        for member in range(1, LINE):
            settle(axis, member).wait()
            total[:, start : start + cols] += coming[axis][member - 1].astype(F32)
    mixed[...] = total[...].astype(BF)
    for axis in range(AXES):
        for member in range(1, LINE):
            share(axis, member).wait_send()
        rows = send[axis].at[:, pl.ds(1, PLANE - 1)]
        pltpu.make_async_copy(rows, rows, send_sem.at[axis]).wait()
        rows = back[axis].at[pl.ds(LINE, DEVICES - LINE)]
        pltpu.make_async_copy(rows, rows, back_sem.at[axis]).wait()


def experts(normed, state, slot_of, weight_of, w_gate_up, w_down):
    vmem = pl.BlockSpec(memory_space=pltpu.VMEM)
    hbm = pl.BlockSpec(memory_space=pl.ANY)
    wide = [(MSG, cols + LOW) for _, cols in PARTS]
    by_source = [(DEVICES, *w) for w in wide]
    by_place = [(LINE, PLANE, *w) for w in wide]
    sems = pltpu.SemaphoreType.DMA((AXES,))
    pair_sems = pltpu.SemaphoreType.DMA((AXES * (LINE - 1),))
    return pl.pallas_call(
        expert_kernel,
        out_shape=tuple(jax.ShapeDtypeStruct(shape, BF) for shape in [(BLOCK, D), *by_source, *by_place]),
        in_specs=[vmem] * 4 + [hbm] * 2,
        out_specs=(vmem,) + (hbm,) * 6,
        scratch_shapes=[
            *(pltpu.VMEM(shape, BF) for shape in by_place),
            *(pltpu.VMEM(shape, BF) for shape in by_source),
            *(pltpu.VMEM((LINE, BLOCK, cols), BF) for _, cols in PARTS),
            *(pltpu.VMEM((CHUNK, *w), BF) for w in wide),
            *(pltpu.VMEM((LINE - 1, BLOCK, cols), BF) for _, cols in PARTS),
            *(pltpu.VMEM((LINE - 1, BLOCK, cols), BF) for _, cols in PARTS),
            pltpu.VMEM((D, 2 * FF), BF),
            pltpu.VMEM((FF, D), BF),
            pltpu.VMEM((CHUNK * 12, D), BF),
            pltpu.VMEM((BLOCK, D), F32),
            pltpu.SemaphoreType.DMA((2,)),
            pair_sems, pair_sems, sems, sems, sems,
            pltpu.SemaphoreType.DMA((AXES * LINE,)),
            sems, pair_sems, pair_sems,
        ],
        compiler_params=pltpu.CompilerParams(
            collective_id=1, has_side_effects=True, vmem_limit_bytes=56 << 20
        ),
        name="experts",
    )(normed, state, slot_of, weight_of, w_gate_up, w_down)[0]


def per_device(
    queries, cached, new_entries, lengths, residual, w_out, norm_gain, w_gate_up, w_down, routes, gate_codes
):
    codes = gate_codes[0].astype(F32)
    weight = codes / jnp.sum(codes, axis=-1, keepdims=True)
    choices = jnp.concatenate([routes[0].astype(F32), weight], axis=1).T
    attn_out, state, normed, slot_of, weight_of = attend_and_norm(
        lengths, queries[0, 0], cached[0, 0], new_entries[0, 0], residual[0], norm_gain[None, :], choices, w_out
    )
    mixed = experts(normed, state, slot_of, weight_of, w_gate_up[0], w_down[0])
    return attn_out[None], mixed[None]


def solution(mesh):
    rows = P(("sub", "dev"), "grp", None)
    heads = P("grp", ("sub", "dev"), None, None)
    expert = P(("grp", "sub", "dev"), None, None)
    placed = (
        heads, heads, heads, P(("sub", "dev")), rows, P("grp", None), P(), expert, expert, rows, rows,
    )
    return jax.shard_map(per_device, mesh=mesh, in_specs=placed, out_specs=(rows, rows), check_vma=False)
```

```python
import functools

import jax
import jax.numpy as jnp
from jax import lax
from jax.experimental import pallas as pl
from jax.experimental.pallas import tpu as pltpu
from jax.sharding import PartitionSpec as P

MESH = pl.DeviceIdType.MESH
TOP = 8
D = 2048
FF = 768
HD = 128
HEADS = 8
CACHE = 4096
SPAN = 512
KEYS = CACHE + SPAN
BLOCK = 128
UNIT = 512
TILE = 512
SCALE = HD**-0.5 * 1.4426950408889634
HIDDEN = -1e30
DEVICES = 128
PLANE = 32
LINE = 4
AXES = 3
STRIDE = 11
MSG = 8
PARTS = ((0, 640), (640, 640), (1280, 768))
LOW = 384
CHUNK = 32
CHUNKS = DEVICES // CHUNK
BF = jnp.bfloat16
F32 = jnp.float32


def iota(shape, dim):
    return lax.broadcasted_iota(jnp.int32, shape, dim)


def rem(a, b):
    return lax.rem(jnp.int32(a), jnp.int32(b))


def div(a, b):
    return lax.div(jnp.int32(a), jnp.int32(b))


def place(offset, sign):
    g, s, d = lax.axis_index("grp"), lax.axis_index("sub"), lax.axis_index("dev")
    og, os, ox, oc = offset
    x = rem(div(d, 2) + sign * ox + 4, 4)
    return rem(g + sign * og + 4, 4), rem(s + sign * os + 4, 4), x * 2 + rem(rem(d, 2) + oc, 2)


def along(axis, step):
    return tuple(step if k == axis else 0 for k in range(AXES)) + (0,)


def across(axis, p):
    a, b, c = div(p, 8), rem(div(p, 2), 4), rem(p, 2)
    return ((0, a, b, c), (a, 0, b, c), (a, b, 0, c))[axis]


def source_at(axis, member, p):
    if axis == 0:
        return member * 32 + p
    if axis == 1:
        return div(p, 8) * 32 + member * 8 + rem(p, 8)
    return div(p, 2) * 8 + member * 2 + rem(p, 2)


def member_and_place(axis, source):
    if axis == 0:
        return div(source, 32), rem(source, 32)
    if axis == 1:
        return rem(div(source, 8), 4), div(source, 32) * 8 + rem(source, 8)
    return rem(div(source, 2), 4), div(source, 8) * 2 + rem(source, 2)


def mixed_place(step):
    o = rem(step * STRIDE, PLANE)
    return rem(o, 4) * 8 + rem(div(o, 4), 4) * 2 + div(o, 16)


def dot(a, b):
    return jnp.dot(a, b, preferred_element_type=F32)


def attend_kernel(
    length, q_ref, cached, new, residual, gain, choices, w_hbm,
    out_ref, state_ref, normed_ref, slot_of, weight_of,
    keys, values, queries, scores, probs, peaks, attended, w_ref, sent, arrived, own, lines,
    w_sem, send_sem, recv_sem, line_send, line_recv,
):
    g, s, d = lax.axis_index("grp"), lax.axis_index("sub"), lax.axis_index("dev")
    w_copy = pltpu.make_async_copy(w_hbm, w_ref, w_sem)
    w_copy.start()
    barrier = pltpu.get_barrier_semaphore()
    for axis in range(AXES):
        for step in range(1, LINE):
            pl.semaphore_signal(barrier, inc=1, device_id=place(along(axis, step), 1), device_id_type=MESH)

    ones = jnp.where(iota((TILE, HD), 1) == 0, 1.0, 0.0).astype(BF)

    @pl.loop(0, CACHE // TILE)
    def _(i):
        rows = pl.ds(pl.multiple_of(i * TILE, TILE), TILE)
        keys[0:HD, rows] = cached[rows, 0:HD].T
        unseen = (iota((HD, TILE), 0) == 0) & (i * TILE + iota((HD, TILE), 1) >= length[0])
        keys[HD:, rows] = jnp.where(unseen, HIDDEN, 0.0).astype(BF)
        values[rows, 0:HD] = cached[rows, HD:]
        values[rows, HD:] = ones

    keys[0:HD, CACHE:] = new[:, 0:HD].T
    keys[HD:, CACHE:] = jnp.zeros((HD, SPAN), BF)
    values[CACHE:, 0:HD] = new[:, HD:]
    values[CACHE:, HD:] = ones
    for slot in range(2):
        queries[slot, :, HD:] = jnp.where(iota((UNIT, HD), 1) == 0, 1.0, 0.0).astype(BF)

    def score(step, slot):
        block = rem(g + 1 + step, 4)
        rows = pl.ds(pl.multiple_of(block * BLOCK, BLOCK), BLOCK)
        for k in range(4):
            head = slot * 4 + k
            queries[slot, k * BLOCK : (k + 1) * BLOCK, 0:HD] = q_ref[rows, head * HD : (head + 1) * HD]
        q = queries[slot]
        peak = None
        for j in range(KEYS // TILE):
            tile = dot(q, keys[:, j * TILE : (j + 1) * TILE])
            if j * TILE >= CACHE:
                row = block * BLOCK + rem(iota((UNIT, TILE), 0), BLOCK)
                tile = jnp.where(iota((UNIT, TILE), 1) + (j * TILE - CACHE) <= row, tile, HIDDEN)
            scores[slot, :, j * TILE : (j + 1) * TILE] = tile
            for k in range(TILE // HD):
                part = tile[:, k * HD : (k + 1) * HD]
                peak = part if peak is None else jnp.maximum(peak, part)
        peaks[slot] = jnp.broadcast_to(jnp.max(peak, axis=1, keepdims=True), (UNIT, HD))

    def finish(slot):
        peak = peaks[slot]
        for k in range(KEYS // HD):
            cols = slice(k * HD, (k + 1) * HD)
            probs[:, cols] = jnp.exp2((scores[slot, :, cols] - peak) * SCALE).astype(BF)
        total = dot(probs[...], values[...])
        result = (total[:, 0:HD] / total[:, HD : HD + 1]).astype(BF)
        for k in range(4):
            head = slot * 4 + k
            attended[:, head * HD : (head + 1) * HD] = result[k * BLOCK : (k + 1) * BLOCK]

    def hand_over(step):
        block = rem(g + 1 + step, 4)
        return pltpu.make_async_remote_copy(
            src_ref=sent.at[step], dst_ref=arrived.at[step],
            send_sem=send_sem.at[step], recv_sem=recv_sem.at[step],
            device_id=(block, s, d), device_id_type=MESH,
        )

    def tell(axis, member):
        at = axis * (LINE - 1) + member - 1
        return pltpu.make_async_remote_copy(
            src_ref=choices, dst_ref=lines.at[at],
            send_sem=line_send.at[at], recv_sem=line_recv.at[at],
            device_id=place(along(axis, member), 1), device_id_type=MESH,
        )

    pairs = [(axis, member) for axis in range(AXES) for member in range(1, LINE)]
    score(0, 0)
    w_copy.wait()
    pl.semaphore_wait(barrier, len(pairs))
    for axis, member in pairs:
        tell(axis, member).start()

    @pl.loop(0, 4)
    def _(step):
        score(step, 1)
        finish(0)
        score(jnp.minimum(step + 1, 3), 0)
        finish(1)
        own[...] = dot(attended[...], w_ref[...])

        @pl.when(step < 3)
        def _():
            sent[step] = own[...].astype(BF)
            hand_over(step).start()

    for axis, member in pairs:
        tell(axis, member).wait()
    earlier = jnp.where(iota((BLOCK, BLOCK), 0) < iota((BLOCK, BLOCK), 1), 1.0, 0.0).astype(BF)
    p = iota((PLANE, BLOCK), 0)
    a, b, core = p >> 3, (p >> 1) & 3, (p + d) & 1
    x = div(d, 2)
    for axis in range(AXES):
        z, y, w = ((0, a, b), (a, 0, b), (a, b, 0))[axis]
        expert = (((g + z) & 3) * 32 + ((s + y) & 3) * 8 + ((x + w) & 3) * 2 + core).astype(F32)
        for member in range(LINE):
            chosen = choices[...] if member == 0 else lines[axis * (LINE - 1) + member - 1]
            hit = jnp.zeros((PLANE, BLOCK), F32)
            weight = jnp.zeros((PLANE, BLOCK), F32)
            for j in range(TOP):
                here = chosen[j : j + 1] == expert
                hit = jnp.where(here, 1.0, hit)
                weight = jnp.where(here, chosen[TOP + j : TOP + j + 1], weight)
            rows = slice((axis * LINE + member) * PLANE, (axis * LINE + member + 1) * PLANE)
            slot_of[rows] = jnp.where(hit > 0.0, dot(hit.astype(BF), earlier), -1.0)
            weight_of[rows] = weight
    for step in range(3):
        hand_over(step).wait()
    attn_sum = own[...] + (arrived[0].astype(F32) + (arrived[1].astype(F32) + arrived[2].astype(F32)))
    out_ref[...] = attn_sum.astype(BF)
    state = residual[...].astype(F32) + attn_sum
    state_ref[...] = state
    inverse = lax.rsqrt(jnp.mean(state * state, axis=1, keepdims=True) + 1e-6)
    normed_ref[...] = (state * inverse * gain[...]).astype(BF)


def attend_and_norm(length, queries, cached, new, residual, gain, choices, w_out):
    vmem = pl.BlockSpec(memory_space=pltpu.VMEM)
    block = (BLOCK, D)
    return pl.pallas_call(
        attend_kernel,
        out_shape=(
            jax.ShapeDtypeStruct(block, BF),
            jax.ShapeDtypeStruct(block, F32),
            jax.ShapeDtypeStruct(block, BF),
            jax.ShapeDtypeStruct((AXES * LINE * PLANE, BLOCK), F32),
            jax.ShapeDtypeStruct((AXES * LINE * PLANE, BLOCK), F32),
        ),
        in_specs=[pl.BlockSpec(memory_space=pltpu.SMEM)] + [vmem] * 6 + [pl.BlockSpec(memory_space=pl.ANY)],
        out_specs=(vmem,) * 5,
        scratch_shapes=[
            pltpu.VMEM((2 * HD, KEYS), BF),
            pltpu.VMEM((KEYS, 2 * HD), BF),
            pltpu.VMEM((2, UNIT, 2 * HD), BF),
            pltpu.VMEM((2, UNIT, KEYS), F32),
            pltpu.VMEM((UNIT, KEYS), BF),
            pltpu.VMEM((2, UNIT, HD), F32),
            pltpu.VMEM((BLOCK, HEADS * HD), BF),
            pltpu.VMEM((HEADS * HD, D), BF),
            pltpu.VMEM((3, *block), BF),
            pltpu.VMEM((3, *block), BF),
            pltpu.VMEM(block, F32),
            pltpu.VMEM((AXES * (LINE - 1), 2 * TOP, BLOCK), F32),
            pltpu.SemaphoreType.DMA,
            pltpu.SemaphoreType.DMA((3,)),
            pltpu.SemaphoreType.DMA((3,)),
            pltpu.SemaphoreType.DMA((AXES * (LINE - 1),)),
            pltpu.SemaphoreType.DMA((AXES * (LINE - 1),)),
        ],
        compiler_params=pltpu.CompilerParams(
            collective_id=0, has_side_effects=True, vmem_limit_bytes=56 << 20
        ),
        name="attend_and_norm",
    )(length, queries, cached, new, residual, gain, choices, w_out)


def expert_kernel(
    normed, state, slot_of, weight_of, up_hbm, down_hbm,
    mixed, recv0, recv1, recv2, ret0, ret1, ret2,
    send0, send1, send2, back0, back1, back2, line0, line1, line2, part0, part1, part2,
    out0, out1, out2, in0, in1, in2, w_up, w_down, x_ref, total,
    w_sem, line_send, line_recv, send_sem, recv_sem, back_sem, ret_sem, part_sem, out_sem, in_sem,
):
    recv, ret, send, back = (recv0, recv1, recv2), (ret0, ret1, ret2), (send0, send1, send2), (back0, back1, back2)
    line, part, leaving, coming = (line0, line1, line2), (part0, part1, part2), (out0, out1, out2), (in0, in1, in2)
    up_copy = pltpu.make_async_copy(up_hbm, w_up, w_sem.at[0])
    down_copy = pltpu.make_async_copy(down_hbm, w_down, w_sem.at[1])
    up_copy.start()
    down_copy.start()
    barrier = pltpu.get_barrier_semaphore()

    @pl.loop(1, DEVICES)
    def _(i):
        offset = (div(i, 32), rem(div(i, 8), 4), rem(div(i, 2), 4), rem(i, 2))
        pl.semaphore_signal(barrier, inc=1, device_id=place(offset, 1), device_id_type=MESH)

    rows_of = CHUNK * MSG
    sub = rem(iota((rows_of, BLOCK), 0), MSG).astype(F32)
    first = sub < 4.0
    for axis, (start, cols) in enumerate(PARTS):
        line[axis][0] = normed[:, start : start + cols]

    def flat(values):
        return values.astype(F32).reshape(rows_of, values.shape[2]).astype(BF)

    def stacked(rows):
        return rows.reshape(CHUNK, MSG, rows.shape[1]).astype(BF)

    def widened(rows):
        if rows.shape[1] == LOW:
            return rows
        return jnp.concatenate([rows, jnp.zeros((rows.shape[0], LOW - rows.shape[1]), F32)], axis=1)

    def spread(ref, axis, member):
        rows = ref[pl.ds(pl.multiple_of((axis * LINE + member) * PLANE, PLANE), PLANE), :]
        return jnp.broadcast_to(rows[:, None, :], (PLANE, MSG, BLOCK)).reshape(rows_of, BLOCK)

    def hits(axis, member):
        slot = spread(slot_of, axis, member)
        return slot == sub, first & (slot == sub + 8.0), (~first) & (slot == sub + 4.0)

    def as_one(mask):
        return jnp.where(mask, 1.0, 0.0).astype(BF)

    def share(axis, member):
        at = axis * (LINE - 1) + member - 1
        return pltpu.make_async_remote_copy(
            src_ref=line[axis].at[0], dst_ref=line[axis].at[member],
            send_sem=line_send.at[at], recv_sem=line_recv.at[at],
            device_id=place(along(axis, member), 1), device_id_type=MESH,
        )

    def outward(axis, member, p):
        source = source_at(axis, member, p)
        arrival = recv_sem.at[axis * CHUNKS + div(source, CHUNK)]
        return pltpu.make_async_remote_copy(
            src_ref=send[axis].at[member, p], dst_ref=recv[axis].at[source],
            send_sem=send_sem.at[axis], recv_sem=arrival,
            device_id=place(across(axis, p), 1), device_id_type=MESH,
        ), pltpu.make_async_copy(send[axis].at[member, p], recv[axis].at[source], arrival)

    def homeward(axis, source):
        member, p = member_and_place(axis, source)
        return p, pltpu.make_async_remote_copy(
            src_ref=back[axis].at[source], dst_ref=ret[axis].at[member, p],
            send_sem=back_sem.at[axis], recv_sem=ret_sem.at[axis * LINE + member],
            device_id=place(across(axis, p), -1), device_id_type=MESH,
        ), pltpu.make_async_copy(
            back[axis].at[source], ret[axis].at[member, p], ret_sem.at[axis * LINE + member]
        )

    def go_home(axis, source):
        p, away, here = homeward(axis, source)

        @pl.when(p > 0)
        def _():
            away.start()

        @pl.when(p == 0)
        def _():
            here.start()

    def settle(axis, member):
        at = axis * (LINE - 1) + member - 1
        return pltpu.make_async_remote_copy(
            src_ref=leaving[axis].at[member - 1], dst_ref=coming[axis].at[member - 1],
            send_sem=out_sem.at[at], recv_sem=in_sem.at[at],
            device_id=place(along(axis, member), -1), device_id_type=MESH,
        )

    def take(sources):
        copies = [pltpu.make_async_copy(source, part[axis], part_sem.at[axis]) for axis, source in sources]
        for copy in copies:
            copy.start()
        for copy in copies:
            copy.wait()

    pl.semaphore_wait(barrier, DEVICES - 1)
    for member in range(1, LINE):
        for axis in range(AXES):
            share(axis, member).start()

    def fill(axis, member):
        cols = PARTS[axis][1]
        whole, low, high = hits(axis, member)
        rows = line[axis][member]
        send[axis][member, :, :, 0:cols] = stacked(dot(as_one(whole), rows))
        rest = dot(as_one(low), rows[:, 0:LOW]) + widened(dot(as_one(high), rows[:, LOW:]))
        send[axis][member, :, :, cols:] = stacked(rest)

    def go_out(axis, member, p):
        away, here = outward(axis, member, p)

        @pl.when(p > 0)
        def _():
            away.start()

        @pl.when(p == 0)
        def _():
            here.start()

    def go_out_for(c, step):
        for axis in (1, 2):
            go_out(axis, rem(step, LINE), c * 8 + rem(div(step, LINE) * 3, 8))

    fill(0, 0)

    @pl.loop(0, PLANE)
    def _(step):
        go_out(0, 0, mixed_place(step))

    fill(1, 0)
    fill(2, 0)

    @pl.loop(1, LINE)
    def _(member):
        for axis in range(AXES):
            share(axis, member).wait_recv()
        for axis in (1, 2):
            fill(axis, member)

    @pl.loop(0, PLANE)
    def _(step):
        go_out_for(0, step)

    @pl.loop(1, LINE)
    def _(member):
        fill(0, member)

    @pl.loop(0, PLANE)
    def _(step):
        for c in (1, 3):
            go_out(0, c, mixed_place(step))
            go_out_for(c, step)

    @pl.loop(0, PLANE)
    def _(step):
        go_out(0, 2, mixed_place(step))
        go_out_for(2, step)

    up_copy.wait()
    down_copy.wait()
    total[...] = state[...]
    quarter = CHUNK * 4
    r, k = iota((quarter, rows_of), 1), iota((quarter, rows_of), 0)
    where = (k >> 2) * MSG + (k & 3)
    pick_low, pick_high = as_one(r == where), as_one(r == where + 4)
    r, k = iota((rows_of, quarter), 0), iota((rows_of, quarter), 1)
    where = (k >> 2) * MSG + (k & 3)
    put_low, put_high = as_one(r == where), as_one(r == where + 4)

    @pl.loop(0, CHUNKS)
    def _(turn):
        c = turn + div(turn, 2) * (1 - 2 * rem(turn, 2))
        for axis in range(AXES):
            group = recv[axis].at[pl.ds(c * CHUNK, CHUNK)]
            pltpu.make_async_copy(group, group, recv_sem.at[axis * CHUNKS + c]).wait()
        take([(axis, recv[axis].at[pl.ds(c * CHUNK, CHUNK)]) for axis in range(AXES)])
        for axis, (start, cols) in enumerate(PARTS):
            x_ref[0:rows_of, start : start + cols] = flat(part[axis][:, :, 0:cols])
            rest = flat(part[axis][:, :, cols:])
            x_ref[rows_of:, start : start + LOW] = dot(pick_low, rest).astype(BF)
            x_ref[rows_of:, start + LOW : start + cols] = dot(pick_high, rest[:, 0 : cols - LOW]).astype(BF)
        projected = dot(x_ref[...], w_up[...])
        gate = projected[:, 0:FF]
        hidden = (gate / (1.0 + jnp.exp(-gate)) * projected[:, FF:]).astype(BF)
        result = dot(hidden, w_down[...])
        cut = result[rows_of:].astype(BF)
        for axis, (start, cols) in enumerate(PARTS):
            back[axis][pl.ds(c * CHUNK, CHUNK), :, 0:cols] = stacked(result[0:rows_of, start : start + cols])
            rest = dot(put_low, cut[:, start : start + LOW])
            rest = rest + widened(dot(put_high, cut[:, start + LOW : start + cols]))
            back[axis][pl.ds(c * CHUNK, CHUNK), :, cols:] = stacked(rest)

        @pl.loop(0, PLANE)
        def _(step):
            source = c * CHUNK + mixed_place(step)
            for axis in range(AXES):
                member = member_and_place(axis, source)[0]

                @pl.when(member > 0)
                def _():
                    go_home(axis, source)

    @pl.loop(0, PLANE)
    def _(step):
        p = mixed_place(step)
        for axis in range(AXES):
            go_home(axis, source_at(axis, 0, p))

    def combine(axis, member):
        cols = PARTS[axis][1]
        group = ret[axis].at[member]
        pltpu.make_async_copy(group, group, ret_sem.at[axis * LINE + member]).wait()
        take([(axis, group)])
        weight = spread(weight_of, axis, member)

        def summed(mask, rows):
            exact = jnp.where(mask, weight, 0.0)
            coarse = exact.astype(BF)
            fine = (exact - coarse.astype(F32)).astype(BF)
            both = jnp.concatenate([coarse, fine], axis=1)
            out = lax.dot_general(both, rows, (((0,), (0,)), ((), ())), preferred_element_type=F32)
            return out[0:BLOCK] + out[BLOCK:]

        whole, low, high = hits(axis, member)
        rest = flat(part[axis][:, :, cols:])
        halves = jnp.concatenate([summed(low, rest), summed(high, rest[:, 0 : cols - LOW])], axis=1)
        return summed(whole, flat(part[axis][:, :, 0:cols])) + halves

    @pl.loop(1, LINE)
    def _(member):
        for axis in range(AXES):
            leaving[axis][member - 1] = combine(axis, member).astype(BF)
            settle(axis, member).start()

    for axis, (start, cols) in enumerate(PARTS):
        total[:, start : start + cols] += combine(axis, 0)

    for axis, (start, cols) in enumerate(PARTS):
        for member in range(1, LINE):
            settle(axis, member).wait()
            total[:, start : start + cols] += coming[axis][member - 1].astype(F32)
    mixed[...] = total[...].astype(BF)
    for axis in range(AXES):
        for member in range(1, LINE):
            share(axis, member).wait_send()
        rows = send[axis].at[:, pl.ds(1, PLANE - 1)]
        pltpu.make_async_copy(rows, rows, send_sem.at[axis]).wait()
        rows = back[axis].at[pl.ds(LINE, DEVICES - LINE)]
        pltpu.make_async_copy(rows, rows, back_sem.at[axis]).wait()


def experts(normed, state, slot_of, weight_of, w_gate_up, w_down):
    vmem = pl.BlockSpec(memory_space=pltpu.VMEM)
    hbm = pl.BlockSpec(memory_space=pl.ANY)
    wide = [(MSG, cols + LOW) for _, cols in PARTS]
    by_source = [(DEVICES, *w) for w in wide]
    by_place = [(LINE, PLANE, *w) for w in wide]
    sems = pltpu.SemaphoreType.DMA((AXES,))
    pair_sems = pltpu.SemaphoreType.DMA((AXES * (LINE - 1),))
    return pl.pallas_call(
        expert_kernel,
        out_shape=tuple(jax.ShapeDtypeStruct(shape, BF) for shape in [(BLOCK, D), *by_source, *by_place]),
        in_specs=[vmem] * 4 + [hbm] * 2,
        out_specs=(vmem,) + (hbm,) * 6,
        scratch_shapes=[
            *(pltpu.VMEM(shape, BF) for shape in by_place),
            *(pltpu.VMEM(shape, BF) for shape in by_source),
            *(pltpu.VMEM((LINE, BLOCK, cols), BF) for _, cols in PARTS),
            *(pltpu.VMEM((CHUNK, *w), BF) for w in wide),
            *(pltpu.VMEM((LINE - 1, BLOCK, cols), BF) for _, cols in PARTS),
            *(pltpu.VMEM((LINE - 1, BLOCK, cols), BF) for _, cols in PARTS),
            pltpu.VMEM((D, 2 * FF), BF),
            pltpu.VMEM((FF, D), BF),
            pltpu.VMEM((CHUNK * 12, D), BF),
            pltpu.VMEM((BLOCK, D), F32),
            pltpu.SemaphoreType.DMA((2,)),
            pair_sems, pair_sems, sems,
            pltpu.SemaphoreType.DMA((AXES * CHUNKS,)),
            sems,
            pltpu.SemaphoreType.DMA((AXES * LINE,)),
            sems, pair_sems, pair_sems,
        ],
        compiler_params=pltpu.CompilerParams(
            collective_id=1, has_side_effects=True, vmem_limit_bytes=56 << 20
        ),
        name="experts",
    )(normed, state, slot_of, weight_of, w_gate_up, w_down)[0]


def per_device(
    queries, cached, new_entries, lengths, residual, w_out, norm_gain, w_gate_up, w_down, routes, gate_codes
):
    codes = gate_codes[0].astype(F32)
    weight = codes / jnp.sum(codes, axis=-1, keepdims=True)
    choices = jnp.concatenate([routes[0].astype(F32), weight], axis=1).T
    attn_out, state, normed, slot_of, weight_of = attend_and_norm(
        lengths, queries[0, 0], cached[0, 0], new_entries[0, 0], residual[0], norm_gain[None, :], choices, w_out
    )
    mixed = experts(normed, state, slot_of, weight_of, w_gate_up[0], w_down[0])
    return attn_out[None], mixed[None]


def solution(mesh):
    rows = P(("sub", "dev"), "grp", None)
    heads = P("grp", ("sub", "dev"), None, None)
    expert = P(("grp", "sub", "dev"), None, None)
    placed = (
        heads, heads, heads, P(("sub", "dev")), rows, P("grp", None), P(), expert, expert, rows, rows,
    )
    return jax.shard_map(per_device, mesh=mesh, in_specs=placed, out_specs=(rows, rows), check_vma=False)
```

```python
import functools

import jax
import jax.numpy as jnp
from jax import lax
from jax.experimental import pallas as pl
from jax.experimental.pallas import tpu as pltpu
from jax.sharding import PartitionSpec as P

MESH = pl.DeviceIdType.MESH
TOP = 8
D = 2048
FF = 768
HD = 128
HEADS = 8
CACHE = 4096
SPAN = 512
KEYS = CACHE + SPAN
BLOCK = 128
UNIT = 512
TILE = 512
SCALE = HD**-0.5 * 1.4426950408889634
HIDDEN = -1e30
DEVICES = 128
PLANE = 32
LINE = 4
AXES = 3
STRIDE = 11
MSG = 8
PARTS = ((0, 640), (640, 640), (1280, 768))
LOW = 384
CHUNK = 32
CHUNKS = DEVICES // CHUNK
BF = jnp.bfloat16
F32 = jnp.float32


def iota(shape, dim):
    return lax.broadcasted_iota(jnp.int32, shape, dim)


def rem(a, b):
    return lax.rem(jnp.int32(a), jnp.int32(b))


def div(a, b):
    return lax.div(jnp.int32(a), jnp.int32(b))


def place(offset, sign):
    g, s, d = lax.axis_index("grp"), lax.axis_index("sub"), lax.axis_index("dev")
    og, os, ox, oc = offset
    x = rem(div(d, 2) + sign * ox + 4, 4)
    return rem(g + sign * og + 4, 4), rem(s + sign * os + 4, 4), x * 2 + rem(rem(d, 2) + oc, 2)


def along(axis, step):
    return tuple(step if k == axis else 0 for k in range(AXES)) + (0,)


def across(axis, p):
    a, b, c = div(p, 8), rem(div(p, 2), 4), rem(p, 2)
    return ((0, a, b, c), (a, 0, b, c), (a, b, 0, c))[axis]


def source_at(axis, member, p):
    if axis == 0:
        return member * 32 + p
    if axis == 1:
        return div(p, 8) * 32 + member * 8 + rem(p, 8)
    return div(p, 2) * 8 + member * 2 + rem(p, 2)


def member_and_place(axis, source):
    if axis == 0:
        return div(source, 32), rem(source, 32)
    if axis == 1:
        return rem(div(source, 8), 4), div(source, 32) * 8 + rem(source, 8)
    return rem(div(source, 2), 4), div(source, 8) * 2 + rem(source, 2)


def mixed_place(step):
    o = rem(step * STRIDE, PLANE)
    return rem(o, 4) * 8 + rem(div(o, 4), 4) * 2 + div(o, 16)


def dot(a, b):
    return jnp.dot(a, b, preferred_element_type=F32)


def ahead(step):
    return 1 + step + (1 - div(step, 2)) * (1 - 2 * rem(step, 2))


def attend_kernel(
    length, q_ref, cached, new, residual, gain, choices, w_hbm,
    out_ref, state_ref, normed_ref, slot_of, weight_of,
    keys, values, queries, scores, probs, peaks, attended, w_ref, sent, arrived, own, lines,
    w_sem, send_sem, recv_sem, line_send, line_recv,
):
    g, s, d = lax.axis_index("grp"), lax.axis_index("sub"), lax.axis_index("dev")
    w_copy = pltpu.make_async_copy(w_hbm, w_ref, w_sem)
    w_copy.start()
    barrier = pltpu.get_barrier_semaphore()
    for axis in range(AXES):
        for step in range(1, LINE):
            pl.semaphore_signal(barrier, inc=1, device_id=place(along(axis, step), 1), device_id_type=MESH)

    ones = jnp.where(iota((TILE, HD), 1) == 0, 1.0, 0.0).astype(BF)

    @pl.loop(0, CACHE // TILE)
    def _(i):
        rows = pl.ds(pl.multiple_of(i * TILE, TILE), TILE)
        keys[0:HD, rows] = cached[rows, 0:HD].T
        unseen = (iota((HD, TILE), 0) == 0) & (i * TILE + iota((HD, TILE), 1) >= length[0])
        keys[HD:, rows] = jnp.where(unseen, HIDDEN, 0.0).astype(BF)
        values[rows, 0:HD] = cached[rows, HD:]
        values[rows, HD:] = ones

    keys[0:HD, CACHE:] = new[:, 0:HD].T
    keys[HD:, CACHE:] = jnp.zeros((HD, SPAN), BF)
    values[CACHE:, 0:HD] = new[:, HD:]
    values[CACHE:, HD:] = ones
    for slot in range(2):
        queries[slot, :, HD:] = jnp.where(iota((UNIT, HD), 1) == 0, 1.0, 0.0).astype(BF)

    def score(step, slot):
        block = rem(g + ahead(step), 4)
        rows = pl.ds(pl.multiple_of(block * BLOCK, BLOCK), BLOCK)
        for k in range(4):
            head = slot * 4 + k
            queries[slot, k * BLOCK : (k + 1) * BLOCK, 0:HD] = q_ref[rows, head * HD : (head + 1) * HD]
        q = queries[slot]
        peak = None
        for j in range(KEYS // TILE):
            tile = dot(q, keys[:, j * TILE : (j + 1) * TILE])
            if j * TILE >= CACHE:
                row = block * BLOCK + rem(iota((UNIT, TILE), 0), BLOCK)
                tile = jnp.where(iota((UNIT, TILE), 1) + (j * TILE - CACHE) <= row, tile, HIDDEN)
            scores[slot, :, j * TILE : (j + 1) * TILE] = tile
            for k in range(TILE // HD):
                part = tile[:, k * HD : (k + 1) * HD]
                peak = part if peak is None else jnp.maximum(peak, part)
        peaks[slot] = jnp.broadcast_to(jnp.max(peak, axis=1, keepdims=True), (UNIT, HD))

    def finish(slot):
        peak = peaks[slot]
        for k in range(KEYS // HD):
            cols = slice(k * HD, (k + 1) * HD)
            probs[:, cols] = jnp.exp2((scores[slot, :, cols] - peak) * SCALE).astype(BF)
        total = dot(probs[...], values[...])
        result = (total[:, 0:HD] / total[:, HD : HD + 1]).astype(BF)
        for k in range(4):
            head = slot * 4 + k
            attended[:, head * HD : (head + 1) * HD] = result[k * BLOCK : (k + 1) * BLOCK]

    def hand_over(step):
        block = rem(g + ahead(step), 4)
        return pltpu.make_async_remote_copy(
            src_ref=sent.at[step], dst_ref=arrived.at[step],
            send_sem=send_sem.at[step], recv_sem=recv_sem.at[step],
            device_id=(block, s, d), device_id_type=MESH,
        )

    def tell(axis, member):
        at = axis * (LINE - 1) + member - 1
        return pltpu.make_async_remote_copy(
            src_ref=choices, dst_ref=lines.at[at],
            send_sem=line_send.at[at], recv_sem=line_recv.at[at],
            device_id=place(along(axis, member), 1), device_id_type=MESH,
        )

    pairs = [(axis, member) for axis in range(AXES) for member in range(1, LINE)]
    score(0, 0)
    w_copy.wait()
    pl.semaphore_wait(barrier, len(pairs))
    for axis, member in pairs:
        tell(axis, member).start()

    @pl.loop(0, 4)
    def _(step):
        score(step, 1)
        finish(0)
        score(jnp.minimum(step + 1, 3), 0)
        finish(1)
        own[...] = dot(attended[...], w_ref[...])

        @pl.when(step < 3)
        def _():
            sent[step] = own[...].astype(BF)
            hand_over(step).start()

    for axis, member in pairs:
        tell(axis, member).wait()
    earlier = jnp.where(iota((BLOCK, BLOCK), 0) < iota((BLOCK, BLOCK), 1), 1.0, 0.0).astype(BF)
    p = iota((PLANE, BLOCK), 0)
    a, b, core = p >> 3, (p >> 1) & 3, (p + d) & 1
    x = div(d, 2)
    for axis in range(AXES):
        z, y, w = ((0, a, b), (a, 0, b), (a, b, 0))[axis]
        expert = (((g + z) & 3) * 32 + ((s + y) & 3) * 8 + ((x + w) & 3) * 2 + core).astype(F32)
        for member in range(LINE):
            chosen = choices[...] if member == 0 else lines[axis * (LINE - 1) + member - 1]
            hit = jnp.zeros((PLANE, BLOCK), F32)
            weight = jnp.zeros((PLANE, BLOCK), F32)
            for j in range(TOP):
                here = chosen[j : j + 1] == expert
                hit = jnp.where(here, 1.0, hit)
                weight = jnp.where(here, chosen[TOP + j : TOP + j + 1], weight)
            rows = slice((axis * LINE + member) * PLANE, (axis * LINE + member + 1) * PLANE)
            slot_of[rows] = jnp.where(hit > 0.0, dot(hit.astype(BF), earlier), -1.0)
            weight_of[rows] = weight
    for step in range(3):
        hand_over(step).wait()
    attn_sum = own[...] + (arrived[0].astype(F32) + (arrived[1].astype(F32) + arrived[2].astype(F32)))
    out_ref[...] = attn_sum.astype(BF)
    state = residual[...].astype(F32) + attn_sum
    state_ref[...] = state
    inverse = lax.rsqrt(jnp.mean(state * state, axis=1, keepdims=True) + 1e-6)
    normed_ref[...] = (state * inverse * gain[...]).astype(BF)


def attend_and_norm(length, queries, cached, new, residual, gain, choices, w_out):
    vmem = pl.BlockSpec(memory_space=pltpu.VMEM)
    block = (BLOCK, D)
    return pl.pallas_call(
        attend_kernel,
        out_shape=(
            jax.ShapeDtypeStruct(block, BF),
            jax.ShapeDtypeStruct(block, F32),
            jax.ShapeDtypeStruct(block, BF),
            jax.ShapeDtypeStruct((AXES * LINE * PLANE, BLOCK), F32),
            jax.ShapeDtypeStruct((AXES * LINE * PLANE, BLOCK), F32),
        ),
        in_specs=[pl.BlockSpec(memory_space=pltpu.SMEM)] + [vmem] * 6 + [pl.BlockSpec(memory_space=pl.ANY)],
        out_specs=(vmem,) * 5,
        scratch_shapes=[
            pltpu.VMEM((2 * HD, KEYS), BF),
            pltpu.VMEM((KEYS, 2 * HD), BF),
            pltpu.VMEM((2, UNIT, 2 * HD), BF),
            pltpu.VMEM((2, UNIT, KEYS), F32),
            pltpu.VMEM((UNIT, KEYS), BF),
            pltpu.VMEM((2, UNIT, HD), F32),
            pltpu.VMEM((BLOCK, HEADS * HD), BF),
            pltpu.VMEM((HEADS * HD, D), BF),
            pltpu.VMEM((3, *block), BF),
            pltpu.VMEM((3, *block), BF),
            pltpu.VMEM(block, F32),
            pltpu.VMEM((AXES * (LINE - 1), 2 * TOP, BLOCK), F32),
            pltpu.SemaphoreType.DMA,
            pltpu.SemaphoreType.DMA((3,)),
            pltpu.SemaphoreType.DMA((3,)),
            pltpu.SemaphoreType.DMA((AXES * (LINE - 1),)),
            pltpu.SemaphoreType.DMA((AXES * (LINE - 1),)),
        ],
        compiler_params=pltpu.CompilerParams(
            collective_id=0, has_side_effects=True, vmem_limit_bytes=56 << 20
        ),
        name="attend_and_norm",
    )(length, queries, cached, new, residual, gain, choices, w_out)


def expert_kernel(
    normed, state, slot_of, weight_of, up_hbm, down_hbm,
    mixed, recv0, recv1, recv2, ret0, ret1, ret2,
    send0, send1, send2, back0, back1, back2, line0, line1, line2, part0, part1, part2,
    out0, out1, out2, in0, in1, in2, w_up, w_down, x_ref, total,
    w_sem, line_send, line_recv, send_sem, recv_sem, back_sem, ret_sem, part_sem, out_sem, in_sem,
):
    recv, ret, send, back = (recv0, recv1, recv2), (ret0, ret1, ret2), (send0, send1, send2), (back0, back1, back2)
    line, part, leaving, coming = (line0, line1, line2), (part0, part1, part2), (out0, out1, out2), (in0, in1, in2)
    up_copy = pltpu.make_async_copy(up_hbm, w_up, w_sem.at[0])
    down_copy = pltpu.make_async_copy(down_hbm, w_down, w_sem.at[1])
    up_copy.start()
    down_copy.start()
    barrier = pltpu.get_barrier_semaphore()

    @pl.loop(1, DEVICES)
    def _(i):
        offset = (div(i, 32), rem(div(i, 8), 4), rem(div(i, 2), 4), rem(i, 2))
        pl.semaphore_signal(barrier, inc=1, device_id=place(offset, 1), device_id_type=MESH)

    rows_of = CHUNK * MSG
    sub = rem(iota((rows_of, BLOCK), 0), MSG).astype(F32)
    first = sub < 4.0
    for axis, (start, cols) in enumerate(PARTS):
        line[axis][0] = normed[:, start : start + cols]

    def flat(values):
        return values.astype(F32).reshape(rows_of, values.shape[2]).astype(BF)

    def stacked(rows):
        return rows.reshape(CHUNK, MSG, rows.shape[1]).astype(BF)

    def widened(rows):
        if rows.shape[1] == LOW:
            return rows
        return jnp.concatenate([rows, jnp.zeros((rows.shape[0], LOW - rows.shape[1]), F32)], axis=1)

    def spread(ref, axis, member):
        rows = ref[pl.ds(pl.multiple_of((axis * LINE + member) * PLANE, PLANE), PLANE), :]
        return jnp.broadcast_to(rows[:, None, :], (PLANE, MSG, BLOCK)).reshape(rows_of, BLOCK)

    def hits(axis, member):
        slot = spread(slot_of, axis, member)
        return slot == sub, first & (slot == sub + 8.0), (~first) & (slot == sub + 4.0)

    def as_one(mask):
        return jnp.where(mask, 1.0, 0.0).astype(BF)

    def share(axis, member):
        at = axis * (LINE - 1) + member - 1
        return pltpu.make_async_remote_copy(
            src_ref=line[axis].at[0], dst_ref=line[axis].at[member],
            send_sem=line_send.at[at], recv_sem=line_recv.at[at],
            device_id=place(along(axis, member), 1), device_id_type=MESH,
        )

    def outward(axis, member, p):
        source = source_at(axis, member, p)
        arrival = recv_sem.at[axis * CHUNKS + div(source, CHUNK)]
        return pltpu.make_async_remote_copy(
            src_ref=send[axis].at[member, p], dst_ref=recv[axis].at[source],
            send_sem=send_sem.at[axis], recv_sem=arrival,
            device_id=place(across(axis, p), 1), device_id_type=MESH,
        ), pltpu.make_async_copy(send[axis].at[member, p], recv[axis].at[source], arrival)

    def homeward(axis, source):
        member, p = member_and_place(axis, source)
        return p, pltpu.make_async_remote_copy(
            src_ref=back[axis].at[source], dst_ref=ret[axis].at[member, p],
            send_sem=back_sem.at[axis], recv_sem=ret_sem.at[axis * LINE + member],
            device_id=place(across(axis, p), -1), device_id_type=MESH,
        ), pltpu.make_async_copy(
            back[axis].at[source], ret[axis].at[member, p], ret_sem.at[axis * LINE + member]
        )

    def go_home(axis, source):
        p, away, here = homeward(axis, source)

        @pl.when(p > 0)
        def _():
            away.start()

        @pl.when(p == 0)
        def _():
            here.start()

    def settle(axis, member):
        at = axis * (LINE - 1) + member - 1
        return pltpu.make_async_remote_copy(
            src_ref=leaving[axis].at[member - 1], dst_ref=coming[axis].at[member - 1],
            send_sem=out_sem.at[at], recv_sem=in_sem.at[at],
            device_id=place(along(axis, member), -1), device_id_type=MESH,
        )

    def take(sources):
        copies = [pltpu.make_async_copy(source, part[axis], part_sem.at[axis]) for axis, source in sources]
        for copy in copies:
            copy.start()
        for copy in copies:
            copy.wait()

    pl.semaphore_wait(barrier, DEVICES - 1)
    for member in range(1, LINE):
        for axis in range(AXES):
            share(axis, member).start()

    def fill(axis, member):
        cols = PARTS[axis][1]
        whole, low, high = hits(axis, member)
        rows = line[axis][member]
        send[axis][member, :, :, 0:cols] = stacked(dot(as_one(whole), rows))
        rest = dot(as_one(low), rows[:, 0:LOW]) + widened(dot(as_one(high), rows[:, LOW:]))
        send[axis][member, :, :, cols:] = stacked(rest)

    def go_out(axis, member, p):
        away, here = outward(axis, member, p)

        @pl.when(p > 0)
        def _():
            away.start()

        @pl.when(p == 0)
        def _():
            here.start()

    def go_out_for(c, step):
        for axis in (1, 2):
            go_out(axis, rem(step, LINE), c * 8 + rem(div(step, LINE) * 3, 8))

    fill(0, 0)

    @pl.loop(0, PLANE)
    def _(step):
        go_out(0, 0, mixed_place(step))

    fill(1, 0)
    fill(2, 0)

    @pl.loop(1, LINE)
    def _(member):
        for axis in range(AXES):
            share(axis, member).wait_recv()
        for axis in (1, 2):
            fill(axis, member)

    @pl.loop(0, PLANE)
    def _(step):
        go_out_for(0, step)

    @pl.loop(1, LINE)
    def _(member):
        fill(0, member)

    @pl.loop(0, PLANE)
    def _(step):
        for c in (1, 3):
            go_out(0, c, mixed_place(step))
            go_out_for(c, step)

    @pl.loop(0, PLANE)
    def _(step):
        go_out(0, 2, mixed_place(step))
        go_out_for(2, step)

    up_copy.wait()
    down_copy.wait()
    total[...] = state[...]
    quarter = CHUNK * 4
    r, k = iota((quarter, rows_of), 1), iota((quarter, rows_of), 0)
    where = (k >> 2) * MSG + (k & 3)
    pick_low, pick_high = as_one(r == where), as_one(r == where + 4)
    r, k = iota((rows_of, quarter), 0), iota((rows_of, quarter), 1)
    where = (k >> 2) * MSG + (k & 3)
    put_low, put_high = as_one(r == where), as_one(r == where + 4)

    @pl.loop(0, CHUNKS)
    def _(turn):
        c = turn + div(turn, 2) * (1 - 2 * rem(turn, 2))
        for axis in range(AXES):
            group = recv[axis].at[pl.ds(c * CHUNK, CHUNK)]
            pltpu.make_async_copy(group, group, recv_sem.at[axis * CHUNKS + c]).wait()
        take([(axis, recv[axis].at[pl.ds(c * CHUNK, CHUNK)]) for axis in range(AXES)])
        for axis, (start, cols) in enumerate(PARTS):
            x_ref[0:rows_of, start : start + cols] = flat(part[axis][:, :, 0:cols])
            rest = flat(part[axis][:, :, cols:])
            x_ref[rows_of:, start : start + LOW] = dot(pick_low, rest).astype(BF)
            x_ref[rows_of:, start + LOW : start + cols] = dot(pick_high, rest[:, 0 : cols - LOW]).astype(BF)
        projected = dot(x_ref[...], w_up[...])
        gate = projected[:, 0:FF]
        hidden = (gate / (1.0 + jnp.exp(-gate)) * projected[:, FF:]).astype(BF)
        result = dot(hidden, w_down[...])
        cut = result[rows_of:].astype(BF)
        for axis, (start, cols) in enumerate(PARTS):
            back[axis][pl.ds(c * CHUNK, CHUNK), :, 0:cols] = stacked(result[0:rows_of, start : start + cols])
            rest = dot(put_low, cut[:, start : start + LOW])
            rest = rest + widened(dot(put_high, cut[:, start + LOW : start + cols]))
            back[axis][pl.ds(c * CHUNK, CHUNK), :, cols:] = stacked(rest)

        @pl.loop(0, PLANE)
        def _(step):
            source = c * CHUNK + mixed_place(step)
            for axis in range(AXES):
                member = member_and_place(axis, source)[0]

                @pl.when(member > 0)
                def _():
                    go_home(axis, source)

    @pl.loop(0, PLANE)
    def _(step):
        p = mixed_place(step)
        for axis in range(AXES):
            go_home(axis, source_at(axis, 0, p))

    def combine(axis, member):
        cols = PARTS[axis][1]
        group = ret[axis].at[member]
        pltpu.make_async_copy(group, group, ret_sem.at[axis * LINE + member]).wait()
        take([(axis, group)])
        weight = spread(weight_of, axis, member)

        def summed(mask, rows):
            exact = jnp.where(mask, weight, 0.0)
            coarse = exact.astype(BF)
            fine = (exact - coarse.astype(F32)).astype(BF)
            both = jnp.concatenate([coarse, fine], axis=1)
            out = lax.dot_general(both, rows, (((0,), (0,)), ((), ())), preferred_element_type=F32)
            return out[0:BLOCK] + out[BLOCK:]

        whole, low, high = hits(axis, member)
        rest = flat(part[axis][:, :, cols:])
        halves = jnp.concatenate([summed(low, rest), summed(high, rest[:, 0 : cols - LOW])], axis=1)
        return summed(whole, flat(part[axis][:, :, 0:cols])) + halves

    @pl.loop(1, LINE)
    def _(member):
        for axis in range(AXES):
            leaving[axis][member - 1] = combine(axis, member).astype(BF)
            settle(axis, member).start()

    for axis, (start, cols) in enumerate(PARTS):
        total[:, start : start + cols] += combine(axis, 0)

    for axis, (start, cols) in enumerate(PARTS):
        for member in range(1, LINE):
            settle(axis, member).wait()
            total[:, start : start + cols] += coming[axis][member - 1].astype(F32)
    mixed[...] = total[...].astype(BF)
    for axis in range(AXES):
        for member in range(1, LINE):
            share(axis, member).wait_send()
        rows = send[axis].at[:, pl.ds(1, PLANE - 1)]
        pltpu.make_async_copy(rows, rows, send_sem.at[axis]).wait()
        rows = back[axis].at[pl.ds(LINE, DEVICES - LINE)]
        pltpu.make_async_copy(rows, rows, back_sem.at[axis]).wait()


def experts(normed, state, slot_of, weight_of, w_gate_up, w_down):
    vmem = pl.BlockSpec(memory_space=pltpu.VMEM)
    hbm = pl.BlockSpec(memory_space=pl.ANY)
    wide = [(MSG, cols + LOW) for _, cols in PARTS]
    by_source = [(DEVICES, *w) for w in wide]
    by_place = [(LINE, PLANE, *w) for w in wide]
    sems = pltpu.SemaphoreType.DMA((AXES,))
    pair_sems = pltpu.SemaphoreType.DMA((AXES * (LINE - 1),))
    return pl.pallas_call(
        expert_kernel,
        out_shape=tuple(jax.ShapeDtypeStruct(shape, BF) for shape in [(BLOCK, D), *by_source, *by_place]),
        in_specs=[vmem] * 4 + [hbm] * 2,
        out_specs=(vmem,) + (hbm,) * 6,
        scratch_shapes=[
            *(pltpu.VMEM(shape, BF) for shape in by_place),
            *(pltpu.VMEM(shape, BF) for shape in by_source),
            *(pltpu.VMEM((LINE, BLOCK, cols), BF) for _, cols in PARTS),
            *(pltpu.VMEM((CHUNK, *w), BF) for w in wide),
            *(pltpu.VMEM((LINE - 1, BLOCK, cols), BF) for _, cols in PARTS),
            *(pltpu.VMEM((LINE - 1, BLOCK, cols), BF) for _, cols in PARTS),
            pltpu.VMEM((D, 2 * FF), BF),
            pltpu.VMEM((FF, D), BF),
            pltpu.VMEM((CHUNK * 12, D), BF),
            pltpu.VMEM((BLOCK, D), F32),
            pltpu.SemaphoreType.DMA((2,)),
            pair_sems, pair_sems, sems,
            pltpu.SemaphoreType.DMA((AXES * CHUNKS,)),
            sems,
            pltpu.SemaphoreType.DMA((AXES * LINE,)),
            sems, pair_sems, pair_sems,
        ],
        compiler_params=pltpu.CompilerParams(
            collective_id=1, has_side_effects=True, vmem_limit_bytes=56 << 20
        ),
        name="experts",
    )(normed, state, slot_of, weight_of, w_gate_up, w_down)[0]


def per_device(
    queries, cached, new_entries, lengths, residual, w_out, norm_gain, w_gate_up, w_down, routes, gate_codes
):
    codes = gate_codes[0].astype(F32)
    weight = codes / jnp.sum(codes, axis=-1, keepdims=True)
    choices = jnp.concatenate([routes[0].astype(F32), weight], axis=1).T
    attn_out, state, normed, slot_of, weight_of = attend_and_norm(
        lengths, queries[0, 0], cached[0, 0], new_entries[0, 0], residual[0], norm_gain[None, :], choices, w_out
    )
    mixed = experts(normed, state, slot_of, weight_of, w_gate_up[0], w_down[0])
    return attn_out[None], mixed[None]


def solution(mesh):
    rows = P(("sub", "dev"), "grp", None)
    heads = P("grp", ("sub", "dev"), None, None)
    expert = P(("grp", "sub", "dev"), None, None)
    placed = (
        heads, heads, heads, P(("sub", "dev")), rows, P("grp", None), P(), expert, expert, rows, rows,
    )
    return jax.shard_map(per_device, mesh=mesh, in_specs=placed, out_specs=(rows, rows), check_vma=False)
```
